32 devices in a mesh: dp: 8 (over z, x), fsdp: 4 (over y, core).
Axes of the slice: x: 2, y: 2, z: 4, core: 2. Of those that a mesh axis runs over, the one named last changes fastest.
Arguments:
- tokens: bfloat16 [64, 512, 768], P(('dp', 'fsdp')), may hold values from -6 to 6
- segments: int32 [64, 512], P(('dp', 'fsdp')), may hold values from 0 to 11, never falling along the last dimension, each value on 1 to 256 neighbouring positions
- w_query: bfloat16 [768, 768], P(('dp', 'fsdp')), may hold values from -0.21875 to 0.21875
- w_key: bfloat16 [768, 768], P(('dp', 'fsdp')), may hold values from -0.21875 to 0.21875
- w_value: bfloat16 [768, 768], P(('dp', 'fsdp')), may hold values from -0.21875 to 0.21875
- w_output: bfloat16 [768, 768], P(('dp', 'fsdp')), may hold values from -1.25 to 1.25
- w_inner: bfloat16 [768, 3072], P(('dp', 'fsdp')), may hold values from -0.21875 to 0.21875
- w_outer: bfloat16 [3072, 768], P(('dp', 'fsdp')), may hold values from -0.109375 to 0.109375
- down_query: bfloat16 [768, 8], P(('dp', 'fsdp')), may hold values from -0.21875 to 0.21875
- down_value: bfloat16 [768, 8], P(('dp', 'fsdp')), may hold values from -0.21875 to 0.21875
- up_query: bfloat16 [8, 768], replicated, may hold values from -0.59765625 to 0.59765625
- up_value: bfloat16 [8, 768], replicated, may hold values from -0.59765625 to 0.59765625
- norm1_gain: float32 [768], replicated, may hold values from 0.5 to 1.5
- norm1_shift: float32 [768], replicated, may hold values from -1.5 to 1.5
- norm2_gain: float32 [768], replicated, may hold values from 0.5 to 1.5
- norm2_shift: float32 [768], replicated, may hold values from -1.5 to 1.5
- out_grad: bfloat16 [64, 512, 768], P(('dp', 'fsdp')), may hold values from -6 to 6
Outputs:
- layer_out: bfloat16 [64, 512, 768], P(('dp', 'fsdp'))
- tokens_grad: bfloat16 [64, 512, 768], P(('dp', 'fsdp'))
- up_query_grad: float32 [8, 768], replicated
- up_value_grad: float32 [8, 768], replicated
The draws below stay inside these ranges and needn't reach their ends.
Inputs may be any that keep to these rules, and one draw needn't show every extreme that they name: `segments`: within each packed row the segment numbers never fall; each item spans 1 to 256 positions, and some item spans exactly 256.
All inputs are finite; a program needn't handle non-finite values.
Results may differ from the reference program's by a relative error of at most 0.014.
The reference program's roundings to bfloat16 on the way count: a program that leaves them out, or rounds other values in their place, can miss the bound.
Values may be sent and summed in bfloat16 or wider, within the bound.
A program may use at most 128 MiB of HBM per device.

```python
import math
import jax
import jax.numpy as jnp
import numpy as np
from jax import lax

D = 768
H = 12
HD = 64
FF = 3072
R = 8
SEQ = 512
SEGS = 12
ROWS = 64


def block_scale(rng, extent, split, smallest, top_value):
    def one(dim, shards_of):
        steps = jax.random.uniform(jax.random.fold_in(jax.random.fold_in(rng, 6), dim), (shards_of,), jnp.float32, smallest / len(split), top_value / len(split))
        return jnp.repeat(jnp.exp(steps), extent[dim] // shards_of).reshape((-1,) + (1,) * (len(extent) - dim - 1))

    level = one(*split[0])
    for cut in split[1:]:
        level = level * one(*cut)
    return level


def split_up(count, total, limit, skew):
    portions = [(1 << 20) // math.isqrt(grade ** skew) + 1 for grade in range(2, count + 1)]
    surplus, holding = total - limit - (count - 1), [1] * (count - 1)
    while surplus > 0:
        free = [i for i in range(count - 1) if holding[i] < limit]
        pool, left = sum([portions[i] for i in free]), surplus
        for i in free:
            extra = min(limit - holding[i], max(1, left * portions[i] // pool), surplus)
            holding[i] = holding[i] + extra
            surplus = surplus - extra
    return np.array([limit] + holding)


def ragged(stream_key, number_of, total, reach, skew):
    if number_of == 2:
        one = jax.random.randint(stream_key, (), max(1, total - reach), min(reach, total - 1) + 1)
        return jnp.stack([one, total - one])
    lengths = jnp.asarray(split_up(number_of, total, reach, skew), jnp.int32)
    couples = (number_of - 1) // 2
    source_of, receiver = lengths[1:1 + 2 * couples:2], lengths[2:2 + 2 * couples:2]
    room = jnp.minimum(source_of - 1, reach - receiver)
    shifted = jax.random.randint(jax.random.fold_in(stream_key, 1), (couples,), 0, 1 << 20) % (room + 1)
    lengths = lengths.at[1:1 + 2 * couples:2].set(source_of - shifted).at[2:2 + 2 * couples:2].set(receiver + shifted)
    return lengths[jax.random.permutation(jax.random.fold_in(stream_key, 2), number_of)]


def scatter_about(rng, shape, scale, bound, pieces=(), held_as=jnp.bfloat16):
    drawn = jax.random.normal(rng, shape, jnp.float32) * scale
    if len(pieces) > 0:
        drawn = block_scale(rng, shape, pieces, -0.22, 0.18) * drawn
    return jnp.clip(drawn, min=-bound, max=bound).astype(held_as)


def setup_inputs(seed: int = 0) -> dict:
    keys = jax.random.split(jax.random.key(seed), 18)
    tokens = scatter_about(keys[0], (ROWS, SEQ, D), 1.0, 6.0, ((0, 32),))
    segments = jax.vmap(lambda own: jnp.searchsorted(jnp.cumsum(ragged(own, SEGS, SEQ, SEQ // 2, 2)), jnp.arange(SEQ), side="right"))(jax.random.split(keys[1], ROWS)).reshape((ROWS, SEQ)).astype(jnp.int32)
    w_query = scatter_about(keys[2], (D, D), D ** -0.5, 0.21875, ((0, 32),))
    w_key = scatter_about(keys[3], (D, D), D ** -0.5, 0.21875, ((0, 32),))
    w_value = scatter_about(keys[4], (D, D), D ** -0.5, 0.21875, ((0, 32),))
    w_output = scatter_about(keys[5], (D, D), (D // 32) ** -0.5, 1.25, ((0, 32),))
    w_inner = scatter_about(keys[6], (D, FF), D ** -0.5, 0.21875, ((0, 32),))
    w_outer = scatter_about(keys[7], (FF, D), FF ** -0.5, 0.109375, ((0, 32),))
    down_query = scatter_about(keys[8], (D, R), D ** -0.5, 0.21875, ((0, 32),))
    down_value = scatter_about(keys[9], (D, R), D ** -0.5, 0.21875, ((0, 32),))
    up_query = scatter_about(keys[10], (R, D), 0.1, 0.59765625)
    up_value = scatter_about(keys[11], (R, D), 0.1, 0.59765625)
    norm1_gain = jnp.clip(1.0 + 0.1 * jax.random.normal(keys[12], (D,), jnp.float32), 0.5, 1.5)
    norm1_shift = scatter_about(keys[13], (D,), 0.3, 1.5, (), jnp.float32)
    norm2_gain = jnp.clip(1.0 + 0.1 * jax.random.normal(keys[14], (D,), jnp.float32), 0.5, 1.5)
    norm2_shift = scatter_about(keys[15], (D,), 0.3, 1.5, (), jnp.float32)
    out_grad = scatter_about(keys[16], (ROWS, SEQ, D), 1.0, 6.0, ((0, 32),))
    return {"tokens": tokens, "segments": segments, "w_query": w_query, "w_key": w_key, "w_value": w_value, "w_output": w_output, "w_inner": w_inner, "w_outer": w_outer, "down_query": down_query, "down_value": down_value, "up_query": up_query, "up_value": up_value, "norm1_gain": norm1_gain, "norm1_shift": norm1_shift, "norm2_gain": norm2_gain, "norm2_shift": norm2_shift, "out_grad": out_grad}


@jax.custom_vjp
def low(v):
    return lax.optimization_barrier(v.astype(jnp.bfloat16)).astype(jnp.float32)

@jax.custom_vjp
def low_back(v):
    return v

def low_keep(v):
    return (low(v), None)

def low_pass(kept, grad):
    return (grad,)

def back_keep(v):
    return (v, None)

def back_low(kept, grad):
    return (low(grad),)
low.defvjp(low_keep, low_pass)
low_back.defvjp(back_keep, back_low)

def matmul_high(left, right):
    return jnp.dot(left, right, precision=lax.Precision.HIGHEST, preferred_element_type=jnp.float32)

def gelu_exact(values):
    return jax.nn.gelu(values, approximate=False)

def layer_norm(values, gain, shift):
    center = values - lax.optimization_barrier(jnp.mean(values, axis=-1, keepdims=True))
    spread = lax.optimization_barrier(jnp.mean(center * center, axis=-1, keepdims=True))
    return center * lax.rsqrt(spread + 1e-05) * gain + shift

def forward(inputs, up_q, up_v, mats, seg_rows):
    wq, wk, wv, wo, win, wout, dq_mat, dv_mat, gain1, shift1, gain2, shift2 = mats
    count, length = (inputs.shape[0], inputs.shape[1])
    low_q = low_back(low(matmul_high(inputs, dq_mat)))
    low_v = low_back(low(matmul_high(inputs, dv_mat)))
    queries = low_back(low(matmul_high(inputs, wq) + 2.0 * matmul_high(low_q, up_q)))
    keys_all = low_back(low(matmul_high(inputs, wk)))
    values_all = low_back(low(matmul_high(inputs, wv) + 2.0 * matmul_high(low_v, up_v)))
    q_heads = queries.reshape(count, length, H, HD)
    k_heads = keys_all.reshape(count, length, H, HD)
    v_heads = values_all.reshape(count, length, H, HD)
    scores = jnp.einsum('gqhd,gkhd->ghqk', q_heads, k_heads, precision=lax.Precision.HIGHEST) * 0.125
    scores = low_back(scores)
    same = seg_rows[:, None, :, None] == seg_rows[:, None, None, :]
    probs = jax.nn.softmax(jnp.where(same, scores, -1e+30), axis=-1)
    context = jnp.einsum('ghqk,gkhd->gqhd', low(probs), v_heads, precision=lax.Precision.HIGHEST)
    context = low_back(low(context.reshape(count, length, H * HD)))
    attended = low_back(matmul_high(context, wo))
    hidden1 = layer_norm(inputs + attended, gain1, shift1)
    inner = low_back(matmul_high(low(hidden1), win))
    active = low(gelu_exact(inner))
    branch = low_back(matmul_high(active, wout))
    return layer_norm(hidden1 + branch, gain2, shift2)

def reference(tokens, segments, w_query, w_key, w_value, w_output, w_inner, w_outer, down_query, down_value, up_query, up_value, norm1_gain, norm1_shift, norm2_gain, norm2_shift, out_grad):
    mats = tuple((m.astype(jnp.float32) for m in (w_query, w_key, w_value, w_output, w_inner, w_outer, down_query, down_value, norm1_gain, norm1_shift, norm2_gain, norm2_shift)))
    up_q = up_query.astype(jnp.float32)
    up_v = up_value.astype(jnp.float32)
    group = math.gcd(ROWS, max(1, 4096 // SEQ))
    steps_all = ROWS // group
    inputs_all = tokens.astype(jnp.float32).reshape(steps_all, group, SEQ, D)
    seg_all = segments.reshape(steps_all, group, SEQ)
    grads_all = out_grad.astype(jnp.float32).reshape(steps_all, group, SEQ, D)

    def one_group(carry, items):
        inputs, seg_rows, cotangent = items
        result, pullback = jax.vjp(lambda xin, uq, uv: forward(xin, uq, uv, mats, seg_rows), inputs, up_q, up_v)
        grad_in, grad_q, grad_v = pullback(cotangent)
        return ((carry[0] + grad_q, carry[1] + grad_v), (result.astype(jnp.bfloat16), grad_in.astype(jnp.bfloat16)))
    start = (jnp.zeros((R, D), jnp.float32), jnp.zeros((R, D), jnp.float32))
    (grad_q, grad_v), (results, input_grads) = lax.scan(one_group, start, (inputs_all, seg_all, grads_all))
    return (results.reshape(ROWS, SEQ, D), input_grads.reshape(ROWS, SEQ, D), grad_q, grad_v)
```

```python
import functools

import jax
import jax.numpy as jnp
from jax import lax
from jax.experimental import pallas as pl
from jax.experimental.pallas import tpu as pltpu
from jax.sharding import PartitionSpec as P

MESH = pl.DeviceIdType.MESH
D, H, HD, FF, R, SEQ = 768, 12, 64, 3072, 8, 512
HALF = SEQ // 2
PAIRS = H // 2
BF, F32 = jnp.bfloat16, jnp.float32
AXES = ("dp", "fsdp")


def dot(a, b):
    return lax.dot_general(a, b, (((1,), (0,)), ((), ())), preferred_element_type=F32)


def dot_nt(a, b):
    return lax.dot_general(a, b, (((1,), (1,)), ((), ())), preferred_element_type=F32)


def dot_tn(a, b):
    return lax.dot_general(a, b, (((0,), (0,)), ((), ())), preferred_element_type=F32)


def place():
    dp, fs = lax.axis_index("dp"), lax.axis_index("fsdp")
    return dp // 2, dp % 2, fs // 2, fs % 2


def device(z, x, y, c):
    return (z * 2 + x, y * 2 + c)


def gather_kernel(groups, *refs):
    xs, outs = refs[:groups], refs[groups : 2 * groups]
    ssem, rsem, lsem = refs[2 * groups :]
    z, x, y, c = place()

    def column(x, y, c):
        return (x * 2 + y) * 2 + c

    xa, ya = jnp.where(c == 0, x, 1 - x), jnp.where(c == 0, 1 - y, y)
    xb, yb = jnp.where(c == 0, 1 - x, x), jnp.where(c == 0, y, 1 - y)
    near, far, twin = device(z, xa, ya, c), device(z, xb, yb, c), device(z, x, y, 1 - c)
    line = [device((z + d) % 4, x, y, c) for d in (1, 2, 3)]
    barrier = pltpu.get_barrier_semaphore()
    for other in (*line, near, far, twin):
        pl.semaphore_signal(barrier, 1, device_id=other, device_id_type=MESH)
    pl.semaphore_wait(barrier, 6)
    mine, at_near, at_far, at_diag = column(x, y, c), column(xa, ya, c), column(xb, yb, c), column(1 - x, 1 - y, c)

    def remote(g, src, dst, k, to):
        pltpu.make_async_remote_copy(
            src_ref=src, dst_ref=dst, send_sem=ssem.at[g], recv_sem=rsem.at[g, k], device_id=to, device_id_type=MESH
        ).start()

    def wait(ref, sem):
        pltpu.make_async_copy(ref, ref, sem).wait()

    def pass_on(g, col, k, to):
        remote(g, outs[g].at[:, col], outs[g].at[:, col], k, to)

    def own(g):
        pltpu.make_async_copy(xs[g], outs[g].at[z, mine], lsem.at[g]).start()
        for d in range(3):
            remote(g, xs[g], outs[g].at[z, mine], d, line[d])

    def after_line(g):
        pltpu.make_async_copy(xs[g], outs[g].at[z, mine], lsem.at[g]).wait()
        for d in range(3):
            wait(xs[g], rsem.at[g, d])
        pass_on(g, mine, 3, near)
        pass_on(g, mine, 4, far)
        pass_on(g, mine, 6, twin)

    def after_near(g):
        wait(outs[g].at[:, at_near], rsem.at[g, 3])
        pass_on(g, at_near, 5, far)
        pass_on(g, at_near, 7, twin)

    def after_far(g):
        wait(outs[g].at[:, at_far], rsem.at[g, 4])
        pass_on(g, at_far, 8, twin)

    def after_diag(g):
        wait(outs[g].at[:, at_diag], rsem.at[g, 5])
        pass_on(g, at_diag, 9, twin)

    stages = (own, after_line, after_near, after_far, after_diag)
    for t in range(groups + len(stages)):
        for k, stage in enumerate(stages):
            if 0 <= t - k < groups:
                stage(t - k)
    for g in range(groups):
        for k in range(4):
            wait(outs[g].at[:, mine], rsem.at[g, 6 + k])
        for _ in range(3):
            wait(xs[g], ssem.at[g])
        for _ in range(7):
            wait(outs[g].at[:, mine], ssem.at[g])


def gather_all(mesh, blocks):
    n = mesh.size
    if dict(mesh.shape) != {"dp": 8, "fsdp": 4} or any(b.shape[0] % 8 for b in blocks):
        return [lax.all_gather(b, AXES, axis=0, tiled=True) for b in blocks]
    k = len(blocks)
    got = pl.pallas_call(
        functools.partial(gather_kernel, k),
        out_shape=[jax.ShapeDtypeStruct((4, 8, *b.shape), b.dtype) for b in blocks],
        in_specs=[pl.BlockSpec(memory_space=pl.ANY)] * k,
        out_specs=[pl.BlockSpec(memory_space=pl.ANY)] * k,
        scratch_shapes=[
            pltpu.SemaphoreType.DMA((k,)),
            pltpu.SemaphoreType.DMA((k, 10)),
            pltpu.SemaphoreType.DMA((k,)),
        ],
        compiler_params=pltpu.CompilerParams(collective_id=0, has_side_effects=True),
        name="gather_weights",
    )(*blocks)
    return [g.reshape(n * b.shape[0], b.shape[1]) for g, b in zip(got, blocks)]


def reduce_kernel(q_ref, v_ref, oq_ref, ov_ref, pair, plane, line, ssem, rsem):
    z, x, y, c = place()
    twin = device(z, x, y, 1 - c)
    chips = [(x, 1 - y), (1 - x, y), (1 - x, 1 - y)]
    planes = [(z + d) % 4 for d in (1, 2, 3)]
    barrier = pltpu.get_barrier_semaphore()
    others = [twin] + [device(z, i, j, c) for i, j in chips] + [device(k, x, y, c) for k in planes]
    for other in others:
        pl.semaphore_signal(barrier, 1, device_id=other, device_id_type=MESH)
    pl.semaphore_wait(barrier, 7)

    def copy(src, dst, k, to):
        return pltpu.make_async_remote_copy(
            src_ref=src, dst_ref=dst, send_sem=ssem.at[k], recv_sem=rsem.at[k], device_id=to, device_id_type=MESH
        )

    first = c == 0
    pair[0] = jnp.where(first, v_ref[...], q_ref[...])
    swap = copy(pair.at[0], pair.at[1], 0, twin)
    swap.start()
    swap.wait()
    plane[x * 2 + y] = jnp.where(first, q_ref[...], v_ref[...]) + pair[1]
    sends = [copy(plane.at[x * 2 + y], plane.at[x * 2 + y], 1 + k, device(z, i, j, c)) for k, (i, j) in enumerate(chips)]
    for s in sends:
        s.start()
    for s in sends:
        s.wait()
    line[z] = (plane[0] + plane[1]) + (plane[2] + plane[3])
    sends = [copy(line.at[z], line.at[z], 4 + k, device(to, x, y, c)) for k, to in enumerate(planes)]
    for s in sends:
        s.start()
    for s in sends:
        s.wait()
    pair[2] = (line[0] + line[1]) + (line[2] + line[3])
    swap = copy(pair.at[2], pair.at[3], 7, twin)
    swap.start()
    swap.wait()
    oq_ref[...] = jnp.where(first, pair[2], pair[3])
    ov_ref[...] = jnp.where(first, pair[3], pair[2])


def sum_all(mesh, q, v):
    if dict(mesh.shape) != {"dp": 8, "fsdp": 4}:
        return lax.psum((q, v), AXES)
    shape = jax.ShapeDtypeStruct(q.shape, F32)
    vmem = pl.BlockSpec(memory_space=pltpu.VMEM)
    return pl.pallas_call(
        reduce_kernel,
        out_shape=[shape, shape],
        in_specs=[vmem, vmem],
        out_specs=[vmem, vmem],
        scratch_shapes=[pltpu.VMEM((4, *q.shape), F32)] * 3
        + [pltpu.SemaphoreType.DMA((8,)), pltpu.SemaphoreType.DMA((8,))],
        compiler_params=pltpu.CompilerParams(collective_id=1, has_side_effects=True),
        name="sum_grads",
    )(q, v)


def gelu_parts(u):
    dens = jnp.exp(u * u * -0.5)
    t = 1.0 / (jnp.abs(u) * (0.3275911 * 0.7071067811865476) + 1.0)
    poly = ((((1.061405429 * t - 1.453152027) * t + 1.421413741) * t - 0.284496736) * t + 0.254829592) * t
    tail = poly * dens * 0.5
    phi = jnp.where(u < 0, tail, 1.0 - tail)
    return u * phi, phi + u * dens * 0.3989422804014327


def layer_kernel(
    seg_ref, x_ref, g_ref, wq, wk, wv, wo, win, wout, down, up_q, up_v, g1, b1, g2, b2,
    y_ref, tg_ref, gq_ref, gv_ref,
    perm_s, permt_s, bias_s, xr_s, low_s, qkv_s, p_s, ctx_s, n1_s, r1_s, hb_s, act_s, gp_s, dz_s, db_s, dqkv_s,
):
    row = pl.program_id(0)
    seg = jnp.broadcast_to(seg_ref[pl.ds(row, 1), :], (8, SEQ))
    lane = lax.broadcasted_iota(jnp.int32, (8, SEQ), 1)
    hit = (seg == pltpu.roll(seg, SEQ - HALF + 1, 1)) & (lane <= HALF)
    a = jnp.min(jnp.where(hit, lane, SEQ), axis=1, keepdims=True)[0:1]
    i = lax.broadcasted_iota(jnp.int32, (SEQ, SEQ), 0)
    j = lax.broadcasted_iota(jnp.int32, (SEQ, SEQ), 1)
    diff = j - i
    perm_s[...] = jnp.where((diff == a) | (diff == a - SEQ), 1.0, 0.0).astype(BF)
    permt_s[...] = jnp.where((diff == -a) | (diff == SEQ - a), 1.0, 0.0).astype(BF)
    segb = seg.astype(F32).astype(BF)
    seg_row = dot_nt(segb, perm_s[HALF:, :])[0:1]
    seg_col = dot_nt(perm_s[HALF:, :], segb)[:, 0:1]
    bias = jnp.where(seg_col == seg_row, 0.0, -1e30)
    bias_s[:, :HALF] = bias
    bias_s[:, HALF:] = bias

    xr_s[...] = dot(perm_s[...], x_ref[0]).astype(BF)
    low_s[...] = dot(xr_s[...], down[...]).astype(BF)

    for n in range(3):
        cols = slice(256 * n, 256 * n + 256)
        q = dot(xr_s[...], wq[:, cols]) + 2.0 * dot(low_s[:, :R], up_q[:, cols])
        v = dot(xr_s[...], wv[:, cols]) + 2.0 * dot(low_s[:, R:], up_v[:, cols])
        qkv_s[:, 256 * n : 256 * n + 256] = q.astype(BF)
        qkv_s[:, D + 256 * n : D + 256 * n + 256] = dot(xr_s[...], wk[:, cols]).astype(BF)
        qkv_s[:, 2 * D + 256 * n : 2 * D + 256 * n + 256] = v.astype(BF)

    low_half = lax.broadcasted_iota(jnp.int32, (HALF, 2 * HD), 1) < HD
    top_half = lax.broadcasted_iota(jnp.int32, (2 * HD, HALF), 0) < HD
    zero = jnp.zeros((HALF, 2 * HD), BF)

    def two(v):
        return jnp.concatenate([jnp.where(low_half, v, zero), jnp.where(low_half, zero, v)], axis=0)

    def pick(v):
        return jnp.where(top_half, v[:, :HALF], v[:, HALF:])

    def heads(p, carry):
        for b in range(2):
            rows = slice(HALF * b, HALF * (b + 1))
            cut = [pl.ds(pl.multiple_of(D * w + 2 * HD * p, 128), 2 * HD) for w in range(3)]
            q, k, v = (qkv_s[rows, c] for c in cut)
            s = dot_nt(k, two(q * 0.125))
            if b == 1:
                s = s + bias_s[...]
            e = jnp.exp(s - jnp.max(s, axis=0, keepdims=True))
            pr = (e * (1.0 / jnp.sum(e, axis=0, keepdims=True))).astype(BF)
            p_s[p, b] = pr
            ctx_s[rows, cut[0]] = pick(dot_tn(v, pr)).T.astype(BF)
        return carry

    lax.fori_loop(0, PAIRS, heads, 0)

    z1 = xr_s[...].astype(F32) + dot(ctx_s[...], wo[...])
    z1 = z1 - jnp.mean(z1, axis=-1, keepdims=True)
    r1 = lax.rsqrt(jnp.mean(z1 * z1, axis=-1, keepdims=True) + 1e-5)
    n1 = z1 * r1
    n1_s[...] = n1
    r1_s[...] = r1
    hb_s[...] = (n1 * g1[...][None] + b1[...][None]).astype(BF)

    def inner(n, carry):
        cols = pl.ds(pl.multiple_of(512 * n, 512), 512)
        act, slope = gelu_parts(dot(hb_s[...], win[:, cols]))
        act_s[:, cols] = act.astype(BF)
        gp_s[:, cols] = slope
        return carry

    lax.fori_loop(0, FF // 512, inner, 0)

    z2 = n1_s[...] * g1[...][None] + b1[...][None] + dot(act_s[...], wout[...])
    z2 = z2 - jnp.mean(z2, axis=-1, keepdims=True)
    r2 = lax.rsqrt(jnp.mean(z2 * z2, axis=-1, keepdims=True) + 1e-5)
    n2 = z2 * r2
    y_ref[0] = dot(permt_s[...], (n2 * g2[...][None] + b2[...][None]).astype(BF)).astype(BF)
    dn2 = dot(perm_s[...], g_ref[0]) * g2[...][None]
    dz2 = r2 * (dn2 - jnp.mean(dn2, axis=-1, keepdims=True) - n2 * jnp.mean(dn2 * n2, axis=-1, keepdims=True))
    dz_s[...] = dz2
    db_s[...] = dz2.astype(BF)

    def inner_back(n, carry):
        cols = pl.ds(pl.multiple_of(512 * n, 512), 512)
        act_s[:, cols] = (dot_nt(db_s[...], wout[cols, :]) * gp_s[:, cols]).astype(BF)
        return carry

    lax.fori_loop(0, FF // 512, inner_back, 0)

    dn1 = (dz_s[...] + dot_nt(act_s[...], win[...])) * g1[...][None]
    n1 = n1_s[...]
    dz1 = r1_s[...] * (dn1 - jnp.mean(dn1, axis=-1, keepdims=True) - n1 * jnp.mean(dn1 * n1, axis=-1, keepdims=True))
    dz_s[...] = dz1
    ctx_s[...] = dot_nt(dz1.astype(BF), wo[...]).astype(BF)

    def heads_back(p, carry):
        for b in range(2):
            rows = slice(HALF * b, HALF * (b + 1))
            cut = [pl.ds(pl.multiple_of(D * w + 2 * HD * p, 128), 2 * HD) for w in range(3)]
            q, k, v = (qkv_s[rows, c] for c in cut)
            dc = two(ctx_s[rows, cut[0]])
            pr = p_s[p, b]
            dqkv_s[rows, cut[2]] = dot(pr, dc).astype(BF)
            dp = dot_nt(v, dc)
            prf = pr.astype(F32)
            ds = (prf * (dp - jnp.sum(prf * dp, axis=0, keepdims=True))).astype(BF)
            dqkv_s[rows, cut[1]] = dot(ds, two(q * 0.125)).astype(BF)
            dqkv_s[rows, cut[0]] = (pick(dot_tn(k, ds)).T * 0.125).astype(BF)
        return carry

    lax.fori_loop(0, PAIRS, heads_back, 0)

    dq, dv = dqkv_s[:, :D], dqkv_s[:, 2 * D :]
    gq = 2.0 * dot_tn(low_s[:, :R], dq)
    gv = 2.0 * dot_tn(low_s[:, R:], dv)
    gq_ref[...] = jnp.where(row == 0, gq, gq_ref[...] + gq)
    gv_ref[...] = jnp.where(row == 0, gv, gv_ref[...] + gv)
    dlow_q = (2.0 * dot_nt(dq, up_q[...])).astype(BF)
    dlow_v = (2.0 * dot_nt(dv, up_v[...])).astype(BF)
    tg = dz_s[...] + dot_nt(dq, wq[...]) + dot_nt(dqkv_s[:, D : 2 * D], wk[...]) + dot_nt(dv, wv[...])
    tg = tg + dot_nt(dlow_q, down[:, :R]) + dot_nt(dlow_v, down[:, R:])
    tg_ref[0] = dot(permt_s[...], tg.astype(BF)).astype(BF)


def run_layer(seg, x, g, wq, wk, wv, wo, win, wout, down, up_q, up_v, g1, b1, g2, b2):
    rows = x.shape[0]

    def whole(v):
        return pl.BlockSpec(v.shape, lambda r: (0,) * v.ndim, pipeline_mode=pl.Buffered(1))

    per_row = pl.BlockSpec((1, SEQ, D), lambda r: (r, 0, 0))
    consts = (wq, wk, wv, wo, win, wout, down, up_q, up_v, g1, b1, g2, b2)
    grad = jax.ShapeDtypeStruct((R, D), F32)
    act = jax.ShapeDtypeStruct(x.shape, BF)
    return pl.pallas_call(
        layer_kernel,
        grid=(rows,),
        out_shape=[act, act, grad, grad],
        in_specs=[whole(seg), per_row, per_row, *map(whole, consts)],
        out_specs=[per_row, per_row] + [pl.BlockSpec((R, D), lambda r: (0, 0))] * 2,
        scratch_shapes=[
            pltpu.VMEM((SEQ, SEQ), BF),
            pltpu.VMEM((SEQ, SEQ), BF),
            pltpu.VMEM((HALF, SEQ), F32),
            pltpu.VMEM((SEQ, D), BF),
            pltpu.VMEM((SEQ, 2 * R), BF),
            pltpu.VMEM((SEQ, 3 * D), BF),
            pltpu.VMEM((PAIRS, 2, HALF, SEQ), BF),
            pltpu.VMEM((SEQ, D), BF),
            pltpu.VMEM((SEQ, D), F32),
            pltpu.VMEM((SEQ, 1), F32),
            pltpu.VMEM((SEQ, D), BF),
            pltpu.VMEM((SEQ, FF), BF),
            pltpu.VMEM((SEQ, FF), F32),
            pltpu.VMEM((SEQ, D), F32),
            pltpu.VMEM((SEQ, D), BF),
            pltpu.VMEM((SEQ, 3 * D), BF),
        ],
        compiler_params=pltpu.CompilerParams(vmem_limit_bytes=60 << 20),
        name="layer_rows",
    )(seg, x, g, *consts)


def solution(mesh):
    def body(
        tokens, segments, w_query, w_key, w_value, w_output, w_inner, w_outer, down_query, down_value,
        up_query, up_value, norm1_gain, norm1_shift, norm2_gain, norm2_shift, out_grad,
    ):
        down = jnp.concatenate([down_query, down_value], axis=1)
        mats = gather_all(mesh, [down, w_query, w_key, w_value, w_output, w_inner, w_outer])
        norms = (norm1_gain, norm1_shift, norm2_gain, norm2_shift)
        y, tg, gq, gv = run_layer(segments, tokens, out_grad, *mats[1:], mats[0], up_query, up_value, *norms)
        gq, gv = sum_all(mesh, gq, gv)
        return y, tg, gq, gv

    split, copied = P(AXES), P()
    return jax.shard_map(
        body,
        mesh=mesh,
        in_specs=(split,) * 10 + (copied,) * 6 + (split,),
        out_specs=(split, split, copied, copied),
        check_vma=False,
    )
```

```python
import functools

import jax
import jax.numpy as jnp
from jax import lax
from jax.experimental import pallas as pl
from jax.experimental.pallas import tpu as pltpu
from jax.sharding import PartitionSpec as P

MESH = pl.DeviceIdType.MESH
D, H, HD, FF, R, SEQ = 768, 12, 64, 3072, 8, 512
HALF, PAIRS, LANES = SEQ // 2, H // 2, 128
WIDE = D + LANES
BF, F32 = jnp.bfloat16, jnp.float32
AXES = ("dp", "fsdp")


def dot(a, b):
    return lax.dot_general(a, b, (((1,), (0,)), ((), ())), preferred_element_type=F32)


def dot_nt(a, b):
    return lax.dot_general(a, b, (((1,), (1,)), ((), ())), preferred_element_type=F32)


def dot_tn(a, b):
    return lax.dot_general(a, b, (((0,), (0,)), ((), ())), preferred_element_type=F32)


def mean(v):
    return jnp.mean(v, axis=-1, keepdims=True)


def gelu_parts(u):
    dens = jnp.exp(u * u * -0.5)
    t = 1.0 / (jnp.abs(u) * (0.3275911 * 0.7071067811865476) + 1.0)
    poly = ((((1.061405429 * t - 1.453152027) * t + 1.421413741) * t - 0.284496736) * t + 0.254829592) * t
    tail = poly * dens * 0.5
    phi = jnp.where(u < 0, tail, 1.0 - tail)
    return u * phi, phi + u * dens * 0.3989422804014327


def two_heads(v):
    first = lax.broadcasted_iota(jnp.int32, v.shape, 1) < HD
    zero = jnp.zeros_like(v)
    return jnp.concatenate([jnp.where(first, v, zero), jnp.where(first, zero, v)], axis=0)


def one_pair(v):
    first = lax.broadcasted_iota(jnp.int32, (2 * HD, HALF), 0) < HD
    return jnp.where(first, v[:, :HALF], v[:, HALF:])


class Links:
    def __init__(self, groups, ssem, rsem, lsem):
        self.groups, self.ssem, self.rsem, self.lsem = groups, ssem, rsem, lsem
        dp, fs = lax.axis_index("dp"), lax.axis_index("fsdp")
        z, x, y, c = self.z, self.x, self.y, self.c = dp // 2, dp % 2, fs // 2, fs % 2
        xa, ya = jnp.where(c == 0, x, 1 - x), jnp.where(c == 0, 1 - y, y)
        xb, yb = jnp.where(c == 0, 1 - x, x), jnp.where(c == 0, y, 1 - y)
        self.near, self.far = self.device(z, xa, ya, c), self.device(z, xb, yb, c)
        self.twin, self.diag = self.device(z, x, y, 1 - c), self.device(z, 1 - x, 1 - y, c)
        self.line = [self.device((z + d) % 4, x, y, c) for d in (1, 2, 3)]
        self.mine, self.at_near = self.column(x, y, c), self.column(xa, ya, c)
        self.at_far, self.at_diag = self.column(xb, yb, c), self.column(1 - x, 1 - y, c)
        self.step, self.done = 0, set()

    @staticmethod
    def device(z, x, y, c):
        return (z * 2 + x, y * 2 + c)

    @staticmethod
    def column(x, y, c):
        return (x * 2 + y) * 2 + c

    def meet(self):
        barrier = pltpu.get_barrier_semaphore()
        others = (*self.line, self.near, self.far, self.diag, self.twin)
        for other in others:
            pl.semaphore_signal(barrier, 1, device_id=other, device_id_type=MESH)
        pl.semaphore_wait(barrier, len(others))

    def slots(self, g, col):
        _, buf, cols = self.groups[g]
        return buf.at[:, col, :, :, cols]

    def slot(self, g):
        _, buf, cols = self.groups[g]
        return buf.at[self.z, self.mine, :, :, cols]

    def remote(self, g, src, dst, k, to):
        pltpu.make_async_remote_copy(
            src_ref=src,
            dst_ref=dst,
            send_sem=self.ssem.at[g],
            recv_sem=self.rsem.at[g, k],
            device_id=to,
            device_id_type=MESH,
        ).start()

    @staticmethod
    def wait(ref, sem):
        pltpu.make_async_copy(ref, ref, sem).wait()

    def pass_on(self, g, col, k, to):
        self.remote(g, self.slots(g, col), self.slots(g, col), k, to)

    def own(self, g):
        src = self.groups[g][0]
        pltpu.make_async_copy(src, self.slot(g), self.lsem.at[g]).start()
        for d in range(3):
            self.remote(g, src, self.slot(g), d, self.line[d])

    def after_line(self, g):
        src = self.groups[g][0]
        pltpu.make_async_copy(src, self.slot(g), self.lsem.at[g]).wait()
        for d in range(3):
            self.wait(src, self.rsem.at[g, d])
        self.pass_on(g, self.mine, 3, self.near)
        self.pass_on(g, self.mine, 4, self.far)
        self.pass_on(g, self.mine, 6, self.twin)

    def after_near(self, g):
        self.wait(self.slots(g, self.at_near), self.rsem.at[g, 3])
        self.pass_on(g, self.at_near, 5, self.far)
        self.pass_on(g, self.at_near, 7, self.twin)

    def after_far(self, g):
        self.wait(self.slots(g, self.at_far), self.rsem.at[g, 4])
        self.pass_on(g, self.at_far, 8, self.twin)

    def after_diag(self, g):
        self.wait(self.slots(g, self.at_diag), self.rsem.at[g, 5])
        self.pass_on(g, self.at_diag, 9, self.twin)

    def tick(self):
        t = self.step
        self.step += 1
        stages = ((0, self.own), (4, self.after_diag), (3, self.after_far), (2, self.after_near), (1, self.after_line))
        for k, stage in stages:
            if 0 <= t - k < len(self.groups):
                stage(t - k)

    def need(self, g):
        while self.step < min(g + 5, len(self.groups) + 4):
            self.tick()
        if g not in self.done:
            self.done.add(g)
            for k in range(4):
                self.wait(self.slots(g, self.mine), self.rsem.at[g, 6 + k])

    def drain(self):
        for g, (src, _, _) in enumerate(self.groups):
            for _ in range(3):
                self.wait(src, self.ssem.at[g])
            for _ in range(7):
                self.wait(self.slots(g, self.mine), self.ssem.at[g])


class Local:
    def __init__(self, groups, lsem):
        self.groups, self.lsem, self.done = groups, lsem, set()
        for g, (src, buf, cols) in enumerate(groups):
            pltpu.make_async_copy(src, buf.at[:, :, :, :, cols], lsem.at[g]).start()

    def tick(self):
        pass

    def need(self, g):
        if g not in self.done:
            self.done.add(g)
            src, buf, cols = self.groups[g]
            pltpu.make_async_copy(src, buf.at[:, :, :, :, cols], self.lsem.at[g]).wait()

    def drain(self):
        pass


class Sums:
    def __init__(self, links, q, v, pair, plane, line, ssem, rsem):
        self.k, self.q, self.v, self.pair, self.plane, self.line = links, q, v, pair, plane, line
        self.ssem, self.rsem = ssem, rsem

    def copy(self, ref, to_ref, k, to):
        return pltpu.make_async_remote_copy(
            src_ref=ref,
            dst_ref=to_ref,
            send_sem=self.ssem.at[k],
            recv_sem=self.rsem.at[k],
            device_id=to,
            device_id_type=MESH,
        )

    def start(self):
        self.pair[0] = jnp.where(self.k.c == 0, self.v[...], self.q[...])
        self.sends = [self.copy(self.pair.at[0], self.pair.at[1], 0, self.k.twin)]
        self.go()

    def go(self):
        for s in self.sends:
            s.start()

    def end(self):
        for s in self.sends:
            s.wait()

    def over_plane(self):
        self.end()
        k = self.k
        here = k.x * 2 + k.y
        self.plane[here] = jnp.where(k.c == 0, self.q[...], self.v[...]) + self.pair[1]
        places = self.plane.at[here]
        self.sends = [self.copy(places, places, 1 + i, to) for i, to in enumerate((k.near, k.far, k.diag))]
        self.go()

    def over_line(self):
        self.end()
        k, p = self.k, self.plane
        self.line[k.z] = (p[0] + p[1]) + (p[2] + p[3])
        places = self.line.at[k.z]
        self.sends = [self.copy(places, places, 4 + i, to) for i, to in enumerate(k.line)]
        self.go()

    def swap(self):
        self.end()
        p = self.line
        self.pair[2] = (p[0] + p[1]) + (p[2] + p[3])
        self.sends = [self.copy(self.pair.at[2], self.pair.at[3], 7, self.k.twin)]
        self.go()

    def finish(self):
        self.end()
        first = self.k.c == 0
        self.q[...] = jnp.where(first, self.pair[2], self.pair[3])
        self.v[...] = jnp.where(first, self.pair[3], self.pair[2])


def layer_kernel(
    remote,
    seg_ref, up_q, up_v, g1, b1, g2, b2, dqt, dvt, x_hbm, g_hbm, wq_h, wk_h, wv_h, wo_h, win_h, wout_h,
    y_hbm, tg_hbm, gq_ref, gv_ref,
    wq_s, wk_s, wv_s, wo_s, win_s, wout_s, own_s, flip_s, up_s,
    x_s, g_s, perm_s, permt_s, bias_s, low_s, qkv_s, p_s, ctx_s, n1_s, r1_s, hb_s, act_s, gp_s, dz_s, db_s, out_s,
    ssem, rsem, lsem, iosem, pair_s, plane_s, line_s, ssem2, rsem2,
):
    rows = range(x_s.shape[0])
    loads = [pltpu.make_async_copy(src, dst, iosem.at[k]) for k, (src, dst) in enumerate(((x_hbm, x_s), (g_hbm, g_s)))]
    for load in loads:
        load.start()

    every, col = slice(None), pl.ds
    groups = [(own_s if remote else wq_h, wq_s, every), (wk_h, wk_s, every), (wv_h, wv_s, every), (wo_h, wo_s, every)]
    lead = (every,) * (2 if remote else 4)
    groups += [(win_h.at[(*lead, col(D * j, D))], win_s, col(D * j, D)) for j in range(4)]
    groups += [(wout_h.at[(*lead, col(HALF * j, HALF))], wout_s, col(HALF * j, HALF)) for j in range(3)]
    wq_g, wk_g, wv_g, wo_g, win_g, wout_g = 0, 1, 2, 3, 4, 8

    if remote:
        stage = pltpu.make_async_copy(wq_h, own_s.at[:, :, col(0, D)], iosem.at[2])
        stage.start()
        flip_s[...] = jnp.zeros_like(flip_s)
        flip_s[0:R, 0 : dqt.shape[1]] = dqt[...].astype(F32)
        flip_s[R : 2 * R, 0 : dvt.shape[1]] = dvt[...].astype(F32)
        downs = flip_s[...].T[0 : dqt.shape[1]].astype(BF)
        own_s[:, :, D:] = downs.reshape(*own_s.shape[:2], LANES)
        net = Links(groups, ssem, rsem, lsem)
        net.meet()
        stage.wait()
    else:
        net = Local(groups, lsem)
    net.tick()
    net.tick()
    zeros = jnp.zeros((R, D), F32)
    up_s[0] = jnp.concatenate([2.0 * up_q[...].astype(F32), zeros], axis=0).astype(BF)
    up_s[1] = jnp.concatenate([zeros, 2.0 * up_v[...].astype(F32)], axis=0).astype(BF)

    def flat(ref, cols=every):
        v = ref[:, :, :, :, cols]
        return v.reshape(-1, v.shape[-1])

    def thirds(fn):
        for n in range(3):
            fn(slice(HALF * n, HALF * (n + 1)))

    def turn(r):
        seg = jnp.broadcast_to(seg_ref[r : r + 1, :], (8, SEQ))
        lane = lax.broadcasted_iota(jnp.int32, (8, SEQ), 1)
        hit = (seg == pltpu.roll(seg, SEQ - HALF + 1, 1)) & (lane <= HALF)
        a = jnp.min(jnp.where(hit, lane, SEQ), axis=1, keepdims=True)[0:1]
        i = lax.broadcasted_iota(jnp.int32, (SEQ, SEQ), 0)
        diff = lax.broadcasted_iota(jnp.int32, (SEQ, SEQ), 1) - i
        perm_s[r] = jnp.where((diff == a) | (diff == a - SEQ), 1.0, 0.0).astype(BF)
        permt_s[r] = jnp.where((diff == -a) | (diff == SEQ - a), 1.0, 0.0).astype(BF)
        segb = seg.astype(F32).astype(BF)
        seg_row = dot_nt(segb, perm_s[r, HALF:, :])[0:1]
        seg_col = dot_nt(perm_s[r, HALF:, :], segb)[:, 0:1]
        bias = jnp.where(seg_col == seg_row, 0.0, -1e30)
        bias_s[r, :, :HALF] = bias
        bias_s[r, :, HALF:] = bias

    def turn_in(ref, r):
        def part(c):
            ref[r, :, c] = dot(perm_s[r], ref[r, :, c]).astype(BF)

        thirds(part)

    def turn_out(value, r, hbm, k):
        out_s[k] = value.astype(BF)

        def part(c):
            out_s[k, :, c] = dot(permt_s[r], out_s[k, :, c]).astype(BF)

        thirds(part)
        put = pltpu.make_async_copy(out_s.at[k], hbm.at[r], iosem.at[3 + k])
        put.start()
        return put

    def project(r):
        low_s[r] = dot(x_s[r], flat(wq_s, slice(D, D + 2 * R))).astype(BF)

        def part(c):
            qkv_s[r, :, c] = (dot(x_s[r], flat(wq_s, c)) + dot(low_s[r], up_s[0, :, c])).astype(BF)

        thirds(part)

    def project_k(r):
        def part(c):
            qkv_s[r, :, D + c.start : D + c.stop] = dot(x_s[r], flat(wk_s, c)).astype(BF)

        thirds(part)

    def project_v(r):
        def part(c):
            v = dot(x_s[r], flat(wv_s, c)) + dot(low_s[r], up_s[1, :, c])
            qkv_s[r, :, 2 * D + c.start : 2 * D + c.stop] = v.astype(BF)

        thirds(part)

    def cuts(p):
        return [slice(D * w + LANES * p, D * w + LANES * (p + 1)) for w in range(3)]

    def heads(r, p):
        cut = cuts(p)
        for b in range(2):
            span = slice(HALF * b, HALF * (b + 1))
            q, k, v = (qkv_s[r, span, c] for c in cut)
            s = dot_nt(k, two_heads(q * 0.125))
            if b == 1:
                s = s + bias_s[r]
            e = jnp.exp(s - jnp.max(s, axis=0, keepdims=True))
            probs = (e * (1.0 / jnp.sum(e, axis=0, keepdims=True))).astype(BF)
            p_s[r, p, b] = probs
            ctx_s[r, span, cut[0]] = one_pair(dot_tn(v, probs)).T.astype(BF)

    def attended(r):
        z1 = x_s[r].astype(F32) + dot(ctx_s[r], flat(wo_s))
        z1 = z1 - mean(z1)
        r1 = lax.rsqrt(mean(z1 * z1) + 1e-5)
        n1 = z1 * r1
        n1_s[r] = n1
        r1_s[r] = r1
        hb_s[r] = (n1 * g1[...][None] + b1[...][None]).astype(BF)

    def inner(r, j):
        for n in range(3):
            c = slice(D * j + HALF * n, D * j + HALF * (n + 1))
            act, slope = gelu_parts(dot(hb_s[r], flat(win_s, c)))
            act_s[r, :, c] = act.astype(BF)
            gp_s[r, :, c] = slope.astype(BF)

    def outer(r, j):
        c = slice(HALF * j, HALF * (j + 1))
        h1 = n1_s[r, :, c] * g1[...][None, c] + b1[...][None, c]
        dz_s[r, :, c] = h1 + dot(act_s[r], flat(wout_s, c))

    def second_norm(r):
        z2 = dz_s[r]
        z2 = z2 - mean(z2)
        r2 = lax.rsqrt(mean(z2 * z2) + 1e-5)
        n2 = z2 * r2
        put = turn_out(n2 * g2[...][None] + b2[...][None], r, y_hbm, r)
        dn2 = g_s[r].astype(F32) * g2[...][None]
        dz2 = r2 * (dn2 - mean(dn2) - n2 * mean(dn2 * n2))
        dz_s[r] = dz2
        db_s[...] = dz2.astype(BF)
        return put

    def inner_back(r):
        for n in range(4):
            c = slice(D * n, D * (n + 1))
            dact = dot_nt(db_s[...], wout_s[n].reshape(D, D))
            act_s[r, :, c] = (dact * gp_s[r, :, c].astype(F32)).astype(BF)

    def first_norm_back(r):
        dn1 = (dz_s[r] + dot_nt(act_s[r], flat(win_s))) * g1[...][None]
        n1 = n1_s[r]
        dz1 = r1_s[r] * (dn1 - mean(dn1) - n1 * mean(dn1 * n1))
        dz_s[r] = dz1
        ctx_s[r] = dot_nt(dz1.astype(BF), flat(wo_s)).astype(BF)

    def heads_back(r, p):
        cut = cuts(p)
        for b in range(2):
            span = slice(HALF * b, HALF * (b + 1))
            q, k, v = (qkv_s[r, span, c] for c in cut)
            dc = two_heads(ctx_s[r, span, cut[0]])
            probs = p_s[r, p, b]
            qkv_s[r, span, cut[2]] = dot(probs, dc).astype(BF)
            dp = dot_nt(v, dc)
            wide = probs.astype(F32)
            ds = (wide * (dp - jnp.sum(wide * dp, axis=0, keepdims=True))).astype(BF)
            qkv_s[r, span, cut[1]] = dot(ds, two_heads(q * 0.125)).astype(BF)
            qkv_s[r, span, cut[0]] = (one_pair(dot_tn(k, ds)).T * 0.125).astype(BF)

    def grads(r):
        gq = 2.0 * dot_tn(low_s[r], qkv_s[r, :, :D])[:R]
        gv = 2.0 * dot_tn(low_s[r], qkv_s[r, :, 2 * D :])[R:]
        gq_ref[...] = gq if r == 0 else gq_ref[...] + gq
        gv_ref[...] = gv if r == 0 else gv_ref[...] + gv

    def tokens_back(r):
        dq, dk, dv = (qkv_s[r, :, D * w : D * (w + 1)] for w in range(3))
        dlow = (dot_nt(dq, up_s[0]) + dot_nt(dv, up_s[1])).astype(BF)
        tg = dz_s[r] + dot_nt(dq, flat(wq_s, slice(0, D))) + dot_nt(dk, flat(wk_s)) + dot_nt(dv, flat(wv_s))
        tg = tg + dot_nt(dlow, flat(wq_s, slice(D, D + 2 * R)))
        return turn_out(tg, r, tg_hbm, r)

    for load in loads:
        load.wait()
    for r in rows:
        turn(r)
        turn_in(x_s, r)
        turn_in(g_s, r)
        net.tick()
    net.need(wq_g)
    for r in rows:
        project(r)
    net.need(wk_g)
    for r in rows:
        project_k(r)
    net.need(wv_g)
    for r in rows:
        project_v(r)
    for r in rows:
        for p in range(PAIRS):
            heads(r, p)
            if p % 3 == 2:
                net.tick()
    net.need(wo_g)
    for r in rows:
        attended(r)
    for j in range(4):
        net.need(win_g + j)
        for r in rows:
            inner(r, j)
    for j in range(3):
        net.need(wout_g + j)
        for r in rows:
            outer(r, j)
    puts = []
    for r in rows:
        puts.append(second_norm(r))
        inner_back(r)
        first_norm_back(r)
    for r in rows:
        for p in range(PAIRS):
            heads_back(r, p)
        grads(r)
    for put in puts:
        put.wait()
    if remote:
        sums = Sums(net, gq_ref, gv_ref, pair_s, plane_s, line_s, ssem2, rsem2)
        sums.start()
    puts = [tokens_back(0)]
    if remote:
        sums.over_plane()
    puts.append(tokens_back(1))
    if remote:
        sums.over_line()
        net.drain()
        sums.swap()
        sums.finish()
    for put in puts:
        put.wait()


def run_layer(remote, seg, x, g, mats, downs, ups, norms):
    rows = x.shape[0]
    vmem, hbm = pl.BlockSpec(memory_space=pltpu.VMEM), pl.BlockSpec(memory_space=pl.ANY)
    act, grad = jax.ShapeDtypeStruct(x.shape, BF), jax.ShapeDtypeStruct((R, D), F32)
    blocks = 11
    shapes = [
        ((4, 8, 3, 8, WIDE), BF),
        ((4, 8, 3, 8, D), BF),
        ((4, 8, 3, 8, D), BF),
        ((4, 8, 3, 8, D), BF),
        ((4, 8, 3, 8, FF), BF),
        ((4, 8, 12, 8, D), BF),
        ((3, 8, WIDE), BF),
        ((LANES, LANES), F32),
        ((2, 2 * R, D), BF),
        ((rows, SEQ, D), BF),
        ((rows, SEQ, D), BF),
        ((rows, SEQ, SEQ), BF),
        ((rows, SEQ, SEQ), BF),
        ((rows, HALF, SEQ), F32),
        ((rows, SEQ, 2 * R), BF),
        ((rows, SEQ, 3 * D), BF),
        ((rows, PAIRS, 2, HALF, SEQ), BF),
        ((rows, SEQ, D), BF),
        ((rows, SEQ, D), F32),
        ((rows, SEQ, 1), F32),
        ((rows, SEQ, D), BF),
        ((rows, SEQ, FF), BF),
        ((rows, SEQ, FF), BF),
        ((rows, SEQ, D), F32),
        ((SEQ, D), BF),
        ((rows, SEQ, D), BF),
    ]
    dma = pltpu.SemaphoreType.DMA
    return pl.pallas_call(
        functools.partial(layer_kernel, remote),
        out_shape=[act, act, grad, grad],
        in_specs=[vmem] * 9 + [hbm] * 8,
        out_specs=[hbm, hbm, vmem, vmem],
        scratch_shapes=[pltpu.VMEM(*s) for s in shapes]
        + [dma((blocks,)), dma((blocks, 10)), dma((blocks,)), dma((5,))]
        + [pltpu.VMEM((4, R, D), F32)] * 3
        + [dma((8,)), dma((8,))],
        compiler_params=pltpu.CompilerParams(
            vmem_limit_bytes=64 << 20,
            **({"collective_id": 0, "has_side_effects": True} if remote else {}),
        ),
        name="layer",
    )(seg, *ups, *norms, *downs, x, g, *mats)


def solution(mesh):
    remote = dict(mesh.shape) == {"dp": 8, "fsdp": 4}

    def body(
        tokens, segments, w_query, w_key, w_value, w_output, w_inner, w_outer, down_query, down_value,
        up_query, up_value, norm1_gain, norm1_shift, norm2_gain, norm2_shift, out_grad,
    ):
        mats = [w_query, w_key, w_value, w_output, w_inner, w_outer]
        if remote:
            mats = [m.reshape(-1, 8, m.shape[1]) for m in mats]
        else:
            pad = jnp.zeros((w_query.shape[0], LANES - 2 * R), BF)
            mats[0] = jnp.concatenate([w_query, down_query, down_value, pad], axis=1)
            mats = [lax.all_gather(m, AXES, axis=0, tiled=True) for m in mats]
            mats = [m.reshape(4, 8, -1, 8, m.shape[1]) for m in mats]
        y, tg, gq, gv = run_layer(
            remote,
            segments,
            tokens,
            out_grad,
            mats,
            (down_query.T, down_value.T),
            (up_query, up_value),
            (norm1_gain, norm1_shift, norm2_gain, norm2_shift),
        )
        if not remote:
            gq, gv = lax.psum((gq, gv), AXES)
        return y, tg, gq, gv

    split, copied = P(AXES), P()
    return jax.shard_map(
        body,
        mesh=mesh,
        in_specs=(split,) * 10 + (copied,) * 6 + (split,),
        out_specs=(split, split, copied, copied),
        check_vma=False,
    )
```

```python
import functools

import jax
import jax.numpy as jnp
from jax import lax
from jax.experimental import pallas as pl
from jax.experimental.pallas import tpu as pltpu
from jax.sharding import PartitionSpec as P

MESH = pl.DeviceIdType.MESH
D, H, HD, FF, R, SEQ = 768, 12, 64, 3072, 8, 512
HALF, PAIRS, LANES = SEQ // 2, H // 2, 128
WIDE = D + LANES
BF, F32 = jnp.bfloat16, jnp.float32
AXES = ("dp", "fsdp")


def dot(a, b):
    return lax.dot_general(a, b, (((1,), (0,)), ((), ())), preferred_element_type=F32)


def dot_nt(a, b):
    return lax.dot_general(a, b, (((1,), (1,)), ((), ())), preferred_element_type=F32)


def dot_tn(a, b):
    return lax.dot_general(a, b, (((0,), (0,)), ((), ())), preferred_element_type=F32)


def mean(v):
    return jnp.mean(v, axis=-1, keepdims=True)


def gelu_parts(u):
    dens = jnp.exp(u * u * -0.5)
    t = 1.0 / (jnp.abs(u) * (0.3275911 * 0.7071067811865476) + 1.0)
    poly = ((((1.061405429 * t - 1.453152027) * t + 1.421413741) * t - 0.284496736) * t + 0.254829592) * t
    tail = poly * dens * 0.5
    phi = jnp.where(u < 0, tail, 1.0 - tail)
    return u * phi, phi + u * dens * 0.3989422804014327


def two_heads(v):
    first = lax.broadcasted_iota(jnp.int32, v.shape, 1) < HD
    zero = jnp.zeros_like(v)
    return jnp.concatenate([jnp.where(first, v, zero), jnp.where(first, zero, v)], axis=0)


def one_pair(v):
    first = lax.broadcasted_iota(jnp.int32, (HALF, 2 * HD), 1) < HD
    return jnp.where(first, v[:HALF], v[HALF:])


def staged(count, *stages):
    held = [None] * count
    for t in range(count + len(stages) - 1):
        for k, stage in enumerate(stages):
            if 0 <= t - k < count:
                held[t - k] = stage(t - k, held[t - k])


class Links:
    def __init__(self, groups, flat, ssem, rsem, lsem):
        self.groups, self.flat, self.ssem, self.rsem, self.lsem = groups, flat, ssem, rsem, lsem
        dp, fs = lax.axis_index("dp"), lax.axis_index("fsdp")
        z, x, y, c = self.z, self.x, self.y, self.c = dp // 2, dp % 2, fs // 2, fs % 2
        xa, ya = jnp.where(c == 0, x, 1 - x), jnp.where(c == 0, 1 - y, y)
        xb, yb = jnp.where(c == 0, 1 - x, x), jnp.where(c == 0, y, 1 - y)
        self.near, self.far = self.device(z, xa, ya, c), self.device(z, xb, yb, c)
        self.twin, self.diag = self.device(z, x, y, 1 - c), self.device(z, 1 - x, 1 - y, c)
        self.line = [self.device((z + d) % 4, x, y, c) for d in (1, 2, 3)]
        self.up, self.down = self.device(jnp.minimum(z + 1, 3), x, y, c), self.device(jnp.maximum(z - 1, 0), x, y, c)
        self.mine, self.at_near, self.at_far, self.at_diag = x * 2 + y, xa * 2 + ya, xb * 2 + yb, 3 - x * 2 - y

    @staticmethod
    def device(z, x, y, c):
        return (z * 2 + x, y * 2 + c)

    def meet(self):
        barrier = pltpu.get_barrier_semaphore()
        others = [to for _, to in self.in_plane()] + self.on_line()[1:]
        for other in others:
            pl.semaphore_signal(barrier, 1, device_id=other, device_id_type=MESH)
        pl.semaphore_wait(barrier, len(others))

    def in_plane(self):
        there = [(n // 4, n // 2 % 2, n % 2) for n in range(1, 8)]
        place = [((self.x + i) % 2, (self.y + j) % 2, (self.c + k) % 2) for i, j, k in there]
        return [(c, self.device(self.z, x, y, c)) for x, y, c in place]

    def on_line(self):
        there = [(0, 1)] + [(d, k) for d in (1, 2, 3) for k in (0, 1)]
        return [self.device((self.z + d) % 4, self.x, self.y, (self.c + k) % 2) for d, k in there]

    def at_column(self, g, chip):
        _, buf, cols = self.groups[g]
        return buf.at[:, chip, self.c, :, :, cols]

    def at_plane(self, g, z):
        _, buf, cols = self.groups[g]
        return buf.at[z, :, self.c, :, :, cols]

    def at_piece(self, g, chip):
        _, buf, cols = self.groups[g]
        return buf.at[self.z, chip, self.c, :, :, cols]

    def send(self, g, src, dst, k, to):
        pltpu.make_async_remote_copy(
            src_ref=src,
            dst_ref=dst,
            send_sem=self.ssem.at[g],
            recv_sem=self.rsem.at[g, k],
            device_id=to,
            device_id_type=MESH,
        ).start()

    @staticmethod
    def wait(ref, sem):
        pltpu.make_async_copy(ref, ref, sem).wait()


    def own(self, g):
        src = self.groups[g][0]
        pltpu.make_async_copy(src, self.at_piece(g, self.mine), self.lsem.at[g]).start()
        for d in range(3):
            self.send(g, src, self.at_piece(g, self.mine), d, self.line[d])

    def column_on(self, g, chip, *to):
        for k, other in to:
            self.send(g, self.at_column(g, chip), self.at_column(g, chip), k, other)

    def after_line(self, g):
        src = self.groups[g][0]
        self.wait(src, self.lsem.at[g])
        for d in range(3):
            self.wait(src, self.rsem.at[g, d])
        self.column_on(g, self.mine, (3, self.near), (4, self.far), (6, self.twin))

    def after_near(self, g):
        self.wait(self.at_column(g, self.at_near), self.rsem.at[g, 3])
        self.column_on(g, self.at_near, (5, self.far), (7, self.twin))

    def after_far(self, g):
        self.wait(self.at_column(g, self.at_far), self.rsem.at[g, 4])
        self.column_on(g, self.at_far, (8, self.twin))

    def after_diag(self, g):
        self.wait(self.at_column(g, self.at_diag), self.rsem.at[g, 5])
        self.column_on(g, self.at_diag, (9, self.twin))

    def whole(self, g):
        for k in range(4):
            self.wait(self.at_column(g, self.mine), self.rsem.at[g, 6 + k])


    def own_flat(self, g):
        src = self.groups[g][0]
        pltpu.make_async_copy(src, self.at_piece(g, self.mine), self.lsem.at[g]).start()
        self.send(g, src, self.at_piece(g, self.mine), 0, self.near)
        self.send(g, src, self.at_piece(g, self.mine), 1, self.far)

    def near_flat(self, g):
        piece = self.at_piece(g, self.at_near)
        self.wait(piece, self.rsem.at[g, 0])
        self.send(g, piece, piece, 2, self.far)

    def plane_on(self, g, z, up, down):
        plane = self.at_plane(g, z)
        if up:
            pl.when(self.z < 3)(lambda: self.send(g, plane, plane, 3 + z, self.up))
        if down:
            pl.when(self.z > 0)(lambda: self.send(g, plane, plane, 3 + z, self.down))
        self.send(g, plane, plane, 7 + z, self.twin)

    def plane_flat(self, g):
        src = self.groups[g][0]
        self.wait(src, self.lsem.at[g])
        self.wait(src, self.rsem.at[g, 1])
        self.wait(src, self.rsem.at[g, 2])
        self.plane_on(g, self.z, True, True)

    def hop_flat(self, d, g):
        def below():
            self.wait(self.at_plane(g, self.z - d), self.rsem.at[g, 3 + self.z - d])
            self.plane_on(g, self.z - d, True, False)

        def above():
            self.wait(self.at_plane(g, self.z + d), self.rsem.at[g, 3 + self.z + d])
            self.plane_on(g, self.z + d, False, True)

        pl.when(self.z >= d)(below)
        pl.when(self.z + d <= 3)(above)

    def whole_flat(self, g):
        for z in range(4):
            self.wait(self.at_plane(g, z), self.rsem.at[g, 7 + z])

    def plan(self):
        first = [g for g in range(len(self.groups)) if g not in self.flat]
        steps = [(self.own, g) for g in first] + [(self.own_flat, g) for g in self.flat]
        stages = (self.after_line, self.after_near, self.after_far, self.after_diag, self.whole)
        main = []
        for t in range(len(first) + len(stages) - 1):
            for k, stage in enumerate(stages):
                if 0 <= t - k < len(first):
                    main.append((stage, first[t - k]))
        side = [self.near_flat, self.plane_flat] + [functools.partial(self.hop_flat, d) for d in (1, 2, 3)]
        when = ((0.12, 0.14), (0.25, 0.30), (0.45, 0.55), (0.65, 0.75), (0.85, 0.95))
        extra = [(f, (stage, g)) for stage, fs in zip(side, when) for f, g in zip(fs, self.flat)]
        for f, item in sorted(extra, key=lambda e: -e[0]):
            main.insert(int(f * len(main)), item)
        return steps, main + [(self.whole_flat, g) for g in self.flat]

    def run(self, works):
        steps, main = self.plan()
        for step, g in steps:
            step(g)
        ends = (self.whole, self.whole_flat)
        here, todo = set(), list(works)
        for step, g in main:
            if todo and todo[0][0] <= here:
                todo.pop(0)[1]()
            step(g)
            if step in ends:
                here.add(g)
        for _, fn in todo:
            fn()

    def drain(self):
        for g, (src, _, _) in enumerate(self.groups):
            for _ in range(3):
                self.wait(src, self.ssem.at[g])
            if g in self.flat:
                plane = self.at_plane(g, 0)
                sent = 4 + jnp.where(self.z < 3, self.z + 1, 0) + jnp.where(self.z > 0, 4 - self.z, 0)
                lax.fori_loop(0, sent, lambda _, v: (self.wait(plane, self.ssem.at[g]), v)[1], 0)
            else:
                for _ in range(7):
                    self.wait(self.at_column(g, self.mine), self.ssem.at[g])


class Local:
    def __init__(self, groups, lsem):
        self.copies = [
            pltpu.make_async_copy(src, buf.at[:, :, :, :, :, cols], lsem.at[g]) for g, (src, buf, cols) in enumerate(groups)
        ]

    def run(self, works):
        for copy in self.copies:
            copy.start()
        here = set()
        for needs, fn in works:
            for g in sorted(needs - here):
                self.copies[g].wait()
            here |= needs
            fn()

    def drain(self):
        pass


class Sums:
    def __init__(self, links, q, v, mine, plane, line, ssem, rsem):
        self.k, self.q, self.v, self.mine, self.plane, self.line = links, q, v, mine, plane, line
        self.ssem, self.rsem, self.sends = ssem, rsem, []

    def copy(self, ref, to_ref, k, to):
        send = pltpu.make_async_remote_copy(
            src_ref=ref,
            dst_ref=to_ref,
            send_sem=self.ssem.at[k],
            recv_sem=self.rsem.at[k],
            device_id=to,
            device_id_type=MESH,
        )
        send.start()
        self.sends.append(send)

    def over_plane(self):
        k = self.k
        slot = self.plane.at[(k.x * 2 + k.y) * 2 + k.c]
        self.mine[0], self.mine[1] = self.q[...], self.v[...]
        self.plane[(k.x * 2 + k.y) * 2 + k.c] = self.mine[k.c]
        for n, (core, to) in enumerate(k.in_plane()):
            self.copy(self.mine.at[core], slot, n, to)

    def end(self):
        for s in self.sends:
            s.wait()
        self.sends = []

    def over_line(self):
        self.end()
        k, p = self.k, self.plane
        self.line[k.c, k.z] = ((p[0] + p[1]) + (p[2] + p[3])) + ((p[4] + p[5]) + (p[6] + p[7]))
        places = self.line.at[k.c, k.z]
        for n, to in enumerate(k.on_line()):
            self.copy(places, places, 7 + n, to)

    def finish(self):
        p = self.line
        for n in range(7):
            pltpu.make_async_copy(p.at[0, 0], p.at[0, 0], self.rsem.at[7 + n]).wait()
            pltpu.make_async_copy(p.at[0, 0], p.at[0, 0], self.ssem.at[7 + n]).wait()
        self.q[...] = (p[0, 0] + p[0, 1]) + (p[0, 2] + p[0, 3])
        self.v[...] = (p[1, 0] + p[1, 1]) + (p[1, 2] + p[1, 3])


def find_turn(seg):
    lane = lax.broadcasted_iota(jnp.int32, (8, SEQ), 1)
    hit = (seg == pltpu.roll(seg, SEQ - HALF + 1, 1)) & (lane <= HALF)
    return jnp.min(jnp.where(hit, lane, SEQ), axis=1, keepdims=True)[0:1]


def turning(by):
    i = lax.broadcasted_iota(jnp.int32, (SEQ, SEQ), 0)
    diff = lax.broadcasted_iota(jnp.int32, (SEQ, SEQ), 1) - i - by
    return jnp.where((diff == 0) | (diff == SEQ) | (diff == -SEQ), 1.0, 0.0).astype(BF)


def layer_kernel(
    remote,
    seg_ref, up_q, up_v, g1, b1, g2, b2, dqt, dvt, x_hbm, g_hbm, wq_h, wk_h, wv_h, wo_h, win_h, wout_h,
    y_hbm, tg_hbm, gq_ref, gv_ref,
    wq_s, wk_s, wv_s, wo_s, win_s, wout_s, own_s, flip_s, up_s,
    x_s, g_s, perm_s, bias_s, low_s, qkv_s, p_s, ctx_s, n1_s, r1_s, hb_s, act_s, gp_s, dz_s, db_s, out_s, two_s,
    ssem, rsem, lsem, iosem, mine_s, plane_s, line_s, ssem2, rsem2,
):
    rows = x_s.shape[0]
    loads = [pltpu.make_async_copy(src, dst, iosem.at[k]) for k, (src, dst) in enumerate(((x_hbm, x_s), (g_hbm, g_s)))]
    for load in loads:
        load.start()

    every, col = slice(None), pl.ds
    groups = [(own_s if remote else wq_h, wq_s, every), (wk_h, wk_s, every), (wv_h, wv_s, every), (wo_h, wo_s, every)]
    lead = (every,) * (2 if remote else 5)
    groups += [(win_h.at[(*lead, col(D * j, D))], win_s, col(D * j, D)) for j in range(4)]
    groups += [(wout_h.at[(*lead, col(HALF * j, HALF))], wout_s, col(HALF * j, HALF)) for j in range(3)]
    wq_g, wk_g, wv_g, wo_g, win_g, wout_g = 0, 1, 2, 3, 4, 8

    if remote:
        stage = pltpu.make_async_copy(wq_h, own_s.at[:, :, col(0, D)], iosem.at[2])
        stage.start()
        flip_s[...] = jnp.zeros_like(flip_s)
        flip_s[0:R, 0 : dqt.shape[1]] = dqt[...].astype(F32)
        flip_s[R : 2 * R, 0 : dvt.shape[1]] = dvt[...].astype(F32)
        downs = flip_s[...].T[0 : dqt.shape[1]].astype(BF)
        own_s[:, :, D:] = downs.reshape(*own_s.shape[:2], LANES)
        net = Links(groups, (wout_g + 1, wout_g + 2), ssem, rsem, lsem)
        net.meet()
        stage.wait()
    else:
        net = Local(groups, lsem)
    zeros = jnp.zeros((R, D), F32)
    up_s[0] = jnp.concatenate([2.0 * up_q[...].astype(F32), zeros], axis=0).astype(BF)
    up_s[1] = jnp.concatenate([zeros, 2.0 * up_v[...].astype(F32)], axis=0).astype(BF)
    gq_ref[...] = jnp.zeros_like(gq_ref)
    gv_ref[...] = jnp.zeros_like(gv_ref)

    def flat(ref, cols=every):
        v = ref[:, :, :, :, :, cols]
        return v.reshape(-1, v.shape[-1])

    def thirds(fn):
        for n in range(3):
            fn(slice(HALF * n, HALF * (n + 1)))

    def each_row(fn, *args):
        def one(r, carry):
            fn(r, *args)
            return carry

        return lambda: lax.fori_loop(0, rows, one, 0)

    def turn(r):
        seg = jnp.broadcast_to(seg_ref[pl.ds(r, 1), :], (8, SEQ))
        perm_s[...] = turning(find_turn(seg))
        segb = seg.astype(F32).astype(BF)
        seg_row = dot_nt(perm_s[HALF:, :], segb)[:, 0:1]
        seg_col = dot_nt(segb, perm_s[HALF:, :])[0:1]
        bias = jnp.where(seg_col == seg_row, 0.0, -1e30)
        bias_s[r, :HALF] = bias
        bias_s[r, HALF:] = bias

        def part(c):
            x_s[r, :, c] = dot(perm_s[...], x_s[r, :, c]).astype(BF)
            g_s[r, :, c] = dot(perm_s[...], g_s[r, :, c]).astype(BF)

        thirds(part)

    def first_turn():
        for load in loads:
            load.wait()
        each_row(turn)()

    def project(r):
        low_s[r] = dot(x_s[r], flat(wq_s, slice(D, D + 2 * R))).astype(BF)

        def part(c):
            qkv_s[r, :, c] = (dot(x_s[r], flat(wq_s, c)) + dot(low_s[r], up_s[0, :, c])).astype(BF)

        thirds(part)

    def project_k(r):
        def part(c):
            qkv_s[r, :, D + c.start : D + c.stop] = dot(x_s[r], flat(wk_s, c)).astype(BF)

        thirds(part)

    def project_v(r):
        def part(c):
            v = dot(x_s[r], flat(wv_s, c)) + dot(low_s[r], up_s[1, :, c])
            qkv_s[r, :, 2 * D + c.start : 2 * D + c.stop] = v.astype(BF)

        thirds(part)

    def item(i, n):
        p, b = 2 * i + n // 2, n % 2
        return p, b, slice(HALF * b, HALF * (b + 1)), [pl.ds(pl.multiple_of(D * w + LANES * p, LANES), LANES) for w in range(3)]

    def heads(r):
        def some(i, carry):
            def scores(n, _):
                p, b, span, cut = item(i, n)
                s = dot_nt(two_heads(qkv_s[r, span, cut[0]] * 0.125), qkv_s[r, span, cut[1]])
                return s + bias_s[r] if b == 1 else s

            def soften(n, s):
                p, b, _, _ = item(i, n)
                e = jnp.exp(s - jnp.max(s, axis=1, keepdims=True))
                probs = (e * (1.0 / jnp.sum(e, axis=1, keepdims=True))).astype(BF)
                p_s[r, p, b] = probs
                return probs

            def context(n, probs):
                p, b, span, cut = item(i, n)
                ctx_s[r, span, cut[0]] = one_pair(dot(probs, qkv_s[r, span, cut[2]])).astype(BF)

            staged(4, scores, soften, context)
            return carry

        lax.fori_loop(0, PAIRS // 2, some, 0)

    def attended(r):
        z1 = x_s[r].astype(F32) + dot(ctx_s[r], flat(wo_s))
        z1 = z1 - mean(z1)
        r1 = lax.rsqrt(mean(z1 * z1) + 1e-5)
        n1 = z1 * r1
        n1_s[r] = n1
        r1_s[r] = r1
        hb_s[r] = (n1 * g1[...][None] + b1[...][None]).astype(BF)

    def inner(r, j):
        for n in range(3):
            c = slice(D * j + HALF * n, D * j + HALF * (n + 1))
            act, slope = gelu_parts(dot(hb_s[r], flat(win_s, c)))
            act_s[r, :, c] = act.astype(BF)
            gp_s[r, :, c] = slope.astype(BF)

    def outer(r, j):
        c = slice(HALF * j, HALF * (j + 1))
        h1 = n1_s[r, :, c] * g1[...][None, c] + b1[...][None, c]
        dz_s[r, :, c] = h1 + dot(act_s[r], flat(wout_s, c))

    def second_norm(r):
        z2 = dz_s[r]
        z2 = z2 - mean(z2)
        r2 = lax.rsqrt(mean(z2 * z2) + 1e-5)
        n2 = z2 * r2
        out_s[r] = (n2 * g2[...][None] + b2[...][None]).astype(BF)
        pltpu.make_async_copy(out_s.at[r], y_hbm.at[r], iosem.at[3]).start()
        dn2 = g_s[r].astype(F32) * g2[...][None]
        dz2 = r2 * (dn2 - mean(dn2) - n2 * mean(dn2 * n2))
        dz_s[r] = dz2
        db_s[...] = dz2.astype(BF)

    def inner_back(r):
        for n in range(4):
            c = slice(D * n, D * (n + 1))
            dact = dot_nt(db_s[...], wout_s[n].reshape(D, D))
            act_s[r, :, c] = (dact * gp_s[r, :, c].astype(F32)).astype(BF)

    def first_norm_back(r):
        dn1 = (dz_s[r] + dot_nt(act_s[r], flat(win_s))) * g1[...][None]
        n1 = n1_s[r]
        dz1 = r1_s[r] * (dn1 - mean(dn1) - n1 * mean(dn1 * n1))
        dz_s[r] = dz1
        ctx_s[r] = dot_nt(dz1.astype(BF), flat(wo_s)).astype(BF)

    def heads_back(t, carry):
        r, i = t // (PAIRS // 2), t % (PAIRS // 2)

        def to(n):
            return slice(HALF * (n % 2), HALF * (n % 2 + 1)), slice(LANES * (n // 2), LANES * (n // 2 + 1))

        def values(n, _):
            p, b, span, cut = item(i, n)
            dc = two_heads(ctx_s[r, span, cut[0]])
            dp = dot_nt(dc, qkv_s[r, span, cut[2]])
            two_s[2, *to(n)] = dot_tn(dc, p_s[r, p, b]).T.astype(BF)
            return dp

        def scores(n, dp):
            p, b, _, _ = item(i, n)
            probs = p_s[r, p, b].astype(F32)
            return (probs * (dp - jnp.sum(probs * dp, axis=1, keepdims=True))).astype(BF)

        def sides(n, ds):
            p, b, span, cut = item(i, n)
            q, k = qkv_s[r, span, cut[0]], qkv_s[r, span, cut[1]]
            two_s[0, *to(n)] = (one_pair(dot(ds, k)) * 0.125).astype(BF)
            two_s[1, *to(n)] = dot_tn(two_heads(q * 0.125), ds).T.astype(BF)

        staged(4, values, scores, sides)
        for w in range(3):
            qkv_s[r, :, pl.ds(pl.multiple_of(D * w + 2 * LANES * i, LANES), 2 * LANES)] = two_s[w]
        return carry

    def grads(r):
        gq_ref[...] += 2.0 * dot_tn(low_s[r], qkv_s[r, :, :D])[:R]
        gv_ref[...] += 2.0 * dot_tn(low_s[r], qkv_s[r, :, 2 * D :])[R:]

    def back(r):
        second_norm(r)
        inner_back(r)
        first_norm_back(r)

    def tokens_back(r):
        dq, dk, dv = (qkv_s[r, :, D * w : D * (w + 1)] for w in range(3))
        dlow = (dot_nt(dq, up_s[0]) + dot_nt(dv, up_s[1])).astype(BF)
        tg = dz_s[r] + dot_nt(dq, flat(wq_s, slice(0, D))) + dot_nt(dk, flat(wk_s)) + dot_nt(dv, flat(wv_s))
        out_s[r] = (tg + dot_nt(dlow, flat(wq_s, slice(D, D + 2 * R)))).astype(BF)
        pltpu.make_async_copy(out_s.at[r], tg_hbm.at[r], iosem.at[4]).start()

    works = [
        (set(), first_turn),
        ({wq_g}, each_row(project)),
        ({wk_g}, each_row(project_k)),
        ({wv_g}, each_row(project_v)),
    ]
    works += [({wv_g}, functools.partial(heads, r)) for r in range(rows)]
    works += [({wo_g}, each_row(attended))]
    works += [({win_g + j}, functools.partial(inner, r, j)) for j in range(4) for r in range(rows)]
    works += [({wout_g + j}, each_row(outer, j)) for j in range(3)]
    net.run(works)
    each_row(back)()
    lax.fori_loop(0, rows * PAIRS // 2, heads_back, 0)
    each_row(grads)()
    pltpu.make_async_copy(out_s, y_hbm, iosem.at[3]).wait()
    if remote:
        sums = Sums(net, gq_ref, gv_ref, mine_s, plane_s, line_s, ssem2, rsem2)
        sums.over_plane()

        def last(r, carry):
            tokens_back(r)
            pl.when(r == 0)(sums.over_line)
            return carry

        lax.fori_loop(0, rows, last, 0)
        net.drain()
        sums.finish()
    else:
        each_row(tokens_back)()
    pltpu.make_async_copy(out_s, tg_hbm, iosem.at[4]).wait()


def unturn_kernel(seg_ref, y_ref, tg_ref, gq_ref, gv_ref, oy_ref, otg_ref, oq_ref, ov_ref, perm_s):
    perm_s[...] = turning(-find_turn(jnp.broadcast_to(seg_ref[pl.ds(pl.program_id(0), 1), :], (8, SEQ))))
    oy_ref[0] = dot(perm_s[...], y_ref[0]).astype(BF)
    otg_ref[0] = dot(perm_s[...], tg_ref[0]).astype(BF)
    oq_ref[...] = gq_ref[...]
    ov_ref[...] = gv_ref[...]


def unturn(seg, y, tg, gq, gv):
    def whole(v):
        return pl.BlockSpec(v.shape, lambda r: (0, 0))

    part = pl.BlockSpec((1, SEQ, D), lambda r: (r, 0, 0))
    act, grad = jax.ShapeDtypeStruct(y.shape, BF), jax.ShapeDtypeStruct(gq.shape, F32)
    return pl.pallas_call(
        unturn_kernel,
        grid=(y.shape[0],),
        out_shape=[act, act, grad, grad],
        in_specs=[whole(seg), part, part, whole(gq), whole(gv)],
        out_specs=[part, part, whole(gq), whole(gv)],
        scratch_shapes=[pltpu.VMEM((SEQ, SEQ), BF)],
        name="unturn",
    )(seg, y, tg, gq, gv)


def run_layer(remote, seg, x, g, mats, downs, ups, norms):
    rows = x.shape[0]
    vmem, hbm = pl.BlockSpec(memory_space=pltpu.VMEM), pl.BlockSpec(memory_space=pl.ANY)
    act, grad = jax.ShapeDtypeStruct(x.shape, BF), jax.ShapeDtypeStruct((R, D), F32)
    blocks = 11
    shapes = [
        ((4, 4, 2, 3, 8, WIDE), BF),
        ((4, 4, 2, 3, 8, D), BF),
        ((4, 4, 2, 3, 8, D), BF),
        ((4, 4, 2, 3, 8, D), BF),
        ((4, 4, 2, 3, 8, FF), BF),
        ((4, 4, 2, 12, 8, D), BF),
        ((3, 8, WIDE), BF),
        ((LANES, LANES), F32),
        ((2, 2 * R, D), BF),
        ((rows, SEQ, D), BF),
        ((rows, SEQ, D), BF),
        ((SEQ, SEQ), BF),
        ((rows, SEQ, HALF), F32),
        ((rows, SEQ, 2 * R), BF),
        ((rows, SEQ, 3 * D), BF),
        ((rows, PAIRS, 2, SEQ, HALF), BF),
        ((rows, SEQ, D), BF),
        ((rows, SEQ, D), F32),
        ((rows, SEQ, 1), F32),
        ((rows, SEQ, D), BF),
        ((rows, SEQ, FF), BF),
        ((rows, SEQ, FF), BF),
        ((rows, SEQ, D), F32),
        ((SEQ, D), BF),
        ((rows, SEQ, D), BF),
        ((3, SEQ, 2 * LANES), BF),
    ]
    dma = pltpu.SemaphoreType.DMA
    return pl.pallas_call(
        functools.partial(layer_kernel, remote),
        out_shape=[act, act, grad, grad],
        in_specs=[vmem] * 9 + [hbm] * 8,
        out_specs=[hbm, hbm, vmem, vmem],
        scratch_shapes=[pltpu.VMEM(*s) for s in shapes]
        + [dma((blocks,)), dma((blocks, 11)), dma((blocks,)), dma((5,))]
        + [pltpu.VMEM((n, R, D), F32) for n in (2, 8)] + [pltpu.VMEM((2, 4, R, D), F32), dma((14,)), dma((14,))],
        compiler_params=pltpu.CompilerParams(
            vmem_limit_bytes=64 << 20,
            **({"collective_id": 0, "has_side_effects": True} if remote else {}),
        ),
        name="layer",
    )(seg, *ups, *norms, *downs, x, g, *mats)


def solution(mesh):
    remote = dict(mesh.shape) == {"dp": 8, "fsdp": 4}

    def body(
        tokens, segments, w_query, w_key, w_value, w_output, w_inner, w_outer, down_query, down_value,
        up_query, up_value, norm1_gain, norm1_shift, norm2_gain, norm2_shift, out_grad,
    ):
        mats = [w_query, w_key, w_value, w_output, w_inner, w_outer]
        if remote:
            mats = [m.reshape(-1, 8, m.shape[1]) for m in mats]
        else:
            pad = jnp.zeros((w_query.shape[0], LANES - 2 * R), BF)
            mats[0] = jnp.concatenate([w_query, down_query, down_value, pad], axis=1)
            mats = [lax.all_gather(m, AXES, axis=0, tiled=True) for m in mats]
            mats = [m.reshape(4, 4, 2, -1, 8, m.shape[1]) for m in mats]
        y, tg, gq, gv = run_layer(
            remote,
            segments,
            tokens,
            out_grad,
            mats,
            (down_query.T, down_value.T),
            (up_query, up_value),
            (norm1_gain, norm1_shift, norm2_gain, norm2_shift),
        )
        if not remote:
            gq, gv = lax.psum((gq, gv), AXES)
        return unturn(segments, y, tg, gq, gv)

    split, copied = P(AXES), P()
    return jax.shard_map(
        body,
        mesh=mesh,
        in_specs=(split,) * 10 + (copied,) * 6 + (split,),
        out_specs=(split, split, copied, copied),
        check_vma=False,
    )
```

```python
import functools

import jax
import jax.numpy as jnp
from jax import lax
from jax.experimental import pallas as pl
from jax.experimental.pallas import tpu as pltpu
from jax.sharding import PartitionSpec as P

MESH = pl.DeviceIdType.MESH
D, H, HD, FF, R, SEQ = 768, 12, 64, 3072, 8, 512
HALF, PAIRS, LANES = SEQ // 2, H // 2, 128
WIDE = D + LANES
BF, F32 = jnp.bfloat16, jnp.float32
AXES = ("dp", "fsdp")


def dot(a, b):
    return lax.dot_general(a, b, (((1,), (0,)), ((), ())), preferred_element_type=F32)


def dot_nt(a, b):
    return lax.dot_general(a, b, (((1,), (1,)), ((), ())), preferred_element_type=F32)


def dot_tn(a, b):
    return lax.dot_general(a, b, (((0,), (0,)), ((), ())), preferred_element_type=F32)


def mean(v):
    return jnp.mean(v, axis=-1, keepdims=True)


def gelu_parts(u):
    dens = jnp.exp(u * u * -0.5)
    t = 1.0 / (jnp.abs(u) * (0.3275911 * 0.7071067811865476) + 1.0)
    poly = ((((1.061405429 * t - 1.453152027) * t + 1.421413741) * t - 0.284496736) * t + 0.254829592) * t
    tail = poly * dens * 0.5
    phi = jnp.where(u < 0, tail, 1.0 - tail)
    return u * phi, phi + u * dens * 0.3989422804014327


def two_heads(v):
    first = lax.broadcasted_iota(jnp.int32, v.shape, 1) < HD
    zero = jnp.zeros_like(v)
    return jnp.concatenate([jnp.where(first, v, zero), jnp.where(first, zero, v)], axis=0)


def one_pair(v):
    first = lax.broadcasted_iota(jnp.int32, (HALF, 2 * HD), 1) < HD
    return jnp.where(first, v[:HALF], v[HALF:])


def staged(count, *stages):
    held = [None] * count
    for t in range(count + len(stages) - 1):
        for k, stage in enumerate(stages):
            if 0 <= t - k < count:
                held[t - k] = stage(t - k, held[t - k])


class Links:
    def __init__(self, groups, flat, early, ssem, rsem, lsem):
        self.early = early
        self.groups, self.flat, self.ssem, self.rsem, self.lsem = groups, flat, ssem, rsem, lsem
        dp, fs = lax.axis_index("dp"), lax.axis_index("fsdp")
        z, x, y, c = self.z, self.x, self.y, self.c = dp // 2, dp % 2, fs // 2, fs % 2
        xa, ya = jnp.where(c == 0, x, 1 - x), jnp.where(c == 0, 1 - y, y)
        xb, yb = jnp.where(c == 0, 1 - x, x), jnp.where(c == 0, y, 1 - y)
        self.near, self.far = self.device(z, xa, ya, c), self.device(z, xb, yb, c)
        self.twin, self.diag = self.device(z, x, y, 1 - c), self.device(z, 1 - x, 1 - y, c)
        self.line = [self.device((z + d) % 4, x, y, c) for d in (1, 2, 3)]
        self.up, self.down = self.device(jnp.minimum(z + 1, 3), x, y, c), self.device(jnp.maximum(z - 1, 0), x, y, c)
        self.mine, self.at_near, self.at_far, self.at_diag = x * 2 + y, xa * 2 + ya, xb * 2 + yb, 3 - x * 2 - y

    @staticmethod
    def device(z, x, y, c):
        return (z * 2 + x, y * 2 + c)

    def meet(self):
        barrier = pltpu.get_barrier_semaphore()
        others = [to for _, to in self.in_plane()] + self.on_line()[1:]
        for other in others:
            pl.semaphore_signal(barrier, 1, device_id=other, device_id_type=MESH)
        pl.semaphore_wait(barrier, len(others))

    def in_plane(self):
        there = [(n // 4, n // 2 % 2, n % 2) for n in range(1, 8)]
        place = [((self.x + i) % 2, (self.y + j) % 2, (self.c + k) % 2) for i, j, k in there]
        return [(c, self.device(self.z, x, y, c)) for x, y, c in place]

    def on_line(self):
        there = [(0, 1)] + [(d, k) for d in (1, 2, 3) for k in (0, 1)]
        return [self.device((self.z + d) % 4, self.x, self.y, (self.c + k) % 2) for d, k in there]

    def at_column(self, g, chip):
        _, buf, cols = self.groups[g]
        return buf.at[:, chip, self.c, :, :, cols]

    def at_plane(self, g, z):
        _, buf, cols = self.groups[g]
        return buf.at[z, :, self.c, :, :, cols]

    def at_piece(self, g, chip):
        _, buf, cols = self.groups[g]
        return buf.at[self.z, chip, self.c, :, :, cols]

    def send(self, g, src, dst, k, to):
        pltpu.make_async_remote_copy(
            src_ref=src,
            dst_ref=dst,
            send_sem=self.ssem.at[g],
            recv_sem=self.rsem.at[g, k],
            device_id=to,
            device_id_type=MESH,
        ).start()

    @staticmethod
    def wait(ref, sem):
        pltpu.make_async_copy(ref, ref, sem).wait()


    def own(self, g):
        src = self.groups[g][0]
        pltpu.make_async_copy(src, self.at_piece(g, self.mine), self.lsem.at[g]).start()
        for d in range(3):
            self.send(g, src, self.at_piece(g, self.mine), d, self.line[d])
        if g in self.early:
            self.send(g, src, self.at_piece(g, self.mine), 3, self.near)
            self.send(g, src, self.at_piece(g, self.mine), 4, self.far)

    def column_on(self, g, chip, *to):
        for k, other in to:
            self.send(g, self.at_column(g, chip), self.at_column(g, chip), k, other)

    def after_line(self, g):
        src = self.groups[g][0]
        self.wait(src, self.lsem.at[g])
        for d in range(3):
            self.wait(src, self.rsem.at[g, d])
        if g in self.early:
            _, buf, cols = self.groups[g]
            for k, other in ((3, self.near), (4, self.far)):
                for d in (1, 2, 3):
                    piece = buf.at[(self.z + d) % 4, self.mine, self.c, :, :, cols]
                    self.send(g, piece, piece, k, other)
            self.column_on(g, self.mine, (6, self.twin))
        else:
            self.column_on(g, self.mine, (3, self.near), (4, self.far), (6, self.twin))

    def after_near(self, g):
        self.wait(self.at_column(g, self.at_near), self.rsem.at[g, 3])
        self.column_on(g, self.at_near, (5, self.far), (7, self.twin))

    def after_far(self, g):
        self.wait(self.at_column(g, self.at_far), self.rsem.at[g, 4])
        self.column_on(g, self.at_far, (8, self.twin))

    def after_diag(self, g):
        self.wait(self.at_column(g, self.at_diag), self.rsem.at[g, 5])
        self.column_on(g, self.at_diag, (9, self.twin))

    def whole(self, g):
        for k in range(4):
            self.wait(self.at_column(g, self.mine), self.rsem.at[g, 6 + k])


    def own_flat(self, g):
        src = self.groups[g][0]
        pltpu.make_async_copy(src, self.at_piece(g, self.mine), self.lsem.at[g]).start()
        self.send(g, src, self.at_piece(g, self.mine), 0, self.near)
        self.send(g, src, self.at_piece(g, self.mine), 1, self.far)

    def near_flat(self, g):
        piece = self.at_piece(g, self.at_near)
        self.wait(piece, self.rsem.at[g, 0])
        self.send(g, piece, piece, 2, self.far)

    def plane_on(self, g, z, up, down):
        plane = self.at_plane(g, z)
        if up:
            pl.when(self.z < 3)(lambda: self.send(g, plane, plane, 3 + z, self.up))
        if down:
            pl.when(self.z > 0)(lambda: self.send(g, plane, plane, 3 + z, self.down))
        self.send(g, plane, plane, 7 + z, self.twin)

    def plane_flat(self, g):
        src = self.groups[g][0]
        self.wait(src, self.lsem.at[g])
        self.wait(src, self.rsem.at[g, 1])
        self.wait(src, self.rsem.at[g, 2])
        self.plane_on(g, self.z, True, True)

    def hop_flat(self, d, g):
        def below():
            self.wait(self.at_plane(g, self.z - d), self.rsem.at[g, 3 + self.z - d])
            self.plane_on(g, self.z - d, True, False)

        def above():
            self.wait(self.at_plane(g, self.z + d), self.rsem.at[g, 3 + self.z + d])
            self.plane_on(g, self.z + d, False, True)

        pl.when(self.z >= d)(below)
        pl.when(self.z + d <= 3)(above)

    def whole_flat(self, g):
        for z in range(4):
            self.wait(self.at_plane(g, z), self.rsem.at[g, 7 + z])

    def plan(self):
        first = [g for g in range(len(self.groups)) if g not in self.flat]
        steps = [(self.own, g) for g in first] + [(self.own_flat, g) for g in self.flat]
        stages = (self.after_line, self.after_near, self.after_far, self.after_diag, self.whole)
        main = []
        for t in range(len(first) + len(stages) - 1):
            for k, stage in enumerate(stages):
                if 0 <= t - k < len(first):
                    main.append((stage, first[t - k]))
        side = [self.near_flat, self.plane_flat] + [functools.partial(self.hop_flat, d) for d in (1, 2, 3)]
        when = ((0.12, 0.14), (0.25, 0.30), (0.45, 0.55), (0.65, 0.75), (0.85, 0.95))
        extra = [(f, (stage, g)) for stage, fs in zip(side, when) for f, g in zip(fs, self.flat)]
        for f, item in sorted(extra, key=lambda e: -e[0]):
            main.insert(int(f * len(main)), item)
        return steps, main + [(self.whole_flat, g) for g in self.flat]

    def run(self, works):
        steps, main = self.plan()
        for step, g in steps:
            step(g)
        ends = (self.whole, self.whole_flat)
        here, todo = set(), list(works)
        for step, g in main:
            if todo and todo[0][0] <= here:
                todo.pop(0)[1]()
            step(g)
            if step in ends:
                here.add(g)
        for _, fn in todo:
            fn()

    def need(self, *groups):
        pass

    def drain(self):
        for g, (src, _, _) in enumerate(self.groups):
            for _ in range(3):
                self.wait(src, self.ssem.at[g])
            if g in self.flat:
                plane = self.at_plane(g, 0)
                sent = 4 + jnp.where(self.z < 3, self.z + 1, 0) + jnp.where(self.z > 0, 4 - self.z, 0)
                lax.fori_loop(0, sent, lambda _, v: (self.wait(plane, self.ssem.at[g]), v)[1], 0)
            else:
                for _ in range(7):
                    self.wait(self.at_column(g, self.mine), self.ssem.at[g])


class Local:
    def __init__(self, groups, lsem):
        self.copies = [
            pltpu.make_async_copy(src, buf.at[:, :, :, :, :, cols], lsem.at[g]) for g, (src, buf, cols) in enumerate(groups)
        ]

    def run(self, works):
        for copy in self.copies:
            copy.start()
        here = set()
        for needs, fn in works:
            for g in sorted(needs - here):
                self.copies[g].wait()
            here |= needs
            fn()

    def need(self, *groups):
        for g in groups:
            self.copies[g].wait()

    def drain(self):
        pass


class Sums:
    def __init__(self, links, q, v, mine, plane, line, ssem, rsem):
        self.k, self.q, self.v, self.mine, self.plane, self.line = links, q, v, mine, plane, line
        self.ssem, self.rsem, self.sends = ssem, rsem, []

    def copy(self, ref, to_ref, k, to):
        send = pltpu.make_async_remote_copy(
            src_ref=ref,
            dst_ref=to_ref,
            send_sem=self.ssem.at[k],
            recv_sem=self.rsem.at[k],
            device_id=to,
            device_id_type=MESH,
        )
        send.start()
        self.sends.append(send)

    def over_plane(self):
        k = self.k
        slot = self.plane.at[(k.x * 2 + k.y) * 2 + k.c]
        self.mine[0], self.mine[1] = self.q[...], self.v[...]
        self.plane[(k.x * 2 + k.y) * 2 + k.c] = self.mine[k.c]
        for n, (core, to) in enumerate(k.in_plane()):
            self.copy(self.mine.at[core], slot, n, to)

    def end(self):
        for s in self.sends:
            s.wait()
        self.sends = []

    def over_line(self):
        self.end()
        k, p = self.k, self.plane
        self.line[k.c, k.z] = ((p[0] + p[1]) + (p[2] + p[3])) + ((p[4] + p[5]) + (p[6] + p[7]))
        places = self.line.at[k.c, k.z]
        for n, to in enumerate(k.on_line()):
            self.copy(places, places, 7 + n, to)

    def finish(self):
        p = self.line
        for n in range(7):
            pltpu.make_async_copy(p.at[0, 0], p.at[0, 0], self.rsem.at[7 + n]).wait()
            pltpu.make_async_copy(p.at[0, 0], p.at[0, 0], self.ssem.at[7 + n]).wait()
        self.q[...] = (p[0, 0] + p[0, 1]) + (p[0, 2] + p[0, 3])
        self.v[...] = (p[1, 0] + p[1, 1]) + (p[1, 2] + p[1, 3])


def find_turn(seg):
    lane = lax.broadcasted_iota(jnp.int32, (8, SEQ), 1)
    hit = (seg == pltpu.roll(seg, SEQ - HALF + 1, 1)) & (lane <= HALF)
    return jnp.min(jnp.where(hit, lane, SEQ), axis=1, keepdims=True)[0:1]


def turning(by):
    i = lax.broadcasted_iota(jnp.int32, (SEQ, SEQ), 0)
    diff = lax.broadcasted_iota(jnp.int32, (SEQ, SEQ), 1) - i - by
    return jnp.where((diff == 0) | (diff == SEQ) | (diff == -SEQ), 1.0, 0.0).astype(BF)


def layer_kernel(
    remote,
    seg_ref, up_q, up_v, g1, b1, g2, b2, dqt, dvt, x_hbm, g_hbm, wq_h, wk_h, wv_h, wo_h, win_h, wout_h,
    y_hbm, tg_hbm, gq_ref, gv_ref,
    wq_s, wk_s, wv_s, wo_s, win_s, wout_s, own_s, flip_s, up_s,
    x_s, g_s, perm_s, bias_s, low_s, qkv_s, p_s, ctx_s, n1_s, r1_s, hb_s, act_s, gp_s, dz_s, out_s, two_s,
    ssem, rsem, lsem, iosem, mine_s, plane_s, line_s, ssem2, rsem2,
):
    rows = x_s.shape[0]
    loads = [pltpu.make_async_copy(src, dst, iosem.at[k]) for k, (src, dst) in enumerate(((x_hbm, x_s), (g_hbm, g_s)))]
    for load in loads:
        load.start()

    every, col = slice(None), pl.ds
    groups = [(own_s if remote else wq_h, wq_s, every), (wk_h, wk_s, every), (wv_h, wv_s, every), (wo_h, wo_s, every)]
    lead = (every,) * (2 if remote else 5)
    groups += [(win_h.at[(*lead, col(D * j, D))], win_s, col(D * j, D)) for j in range(4)]
    groups += [(wout_h.at[(*lead, col(HALF * j, HALF))], wout_s, col(HALF * j, HALF)) for j in range(3)]
    wq_g, wk_g, wv_g, wo_g, win_g, wout_g = 0, 1, 2, 3, 4, 8

    if remote:
        stage = pltpu.make_async_copy(wq_h, own_s.at[:, :, col(0, D)], iosem.at[2])
        stage.start()
        flip_s[...] = jnp.zeros_like(flip_s)
        flip_s[0:R, 0 : dqt.shape[1]] = dqt[...].astype(F32)
        flip_s[R : 2 * R, 0 : dvt.shape[1]] = dvt[...].astype(F32)
        downs = flip_s[...].T[0 : dqt.shape[1]].astype(BF)
        own_s[:, :, D:] = downs.reshape(*own_s.shape[:2], LANES)
        net = Links(groups, (wout_g + 1, wout_g + 2), (0, 1, 2, 3, 4), ssem, rsem, lsem)
        net.meet()
        stage.wait()
    else:
        net = Local(groups, lsem)
    zeros = jnp.zeros((R, D), F32)
    up_s[0] = jnp.concatenate([2.0 * up_q[...].astype(F32), zeros], axis=0).astype(BF)
    up_s[1] = jnp.concatenate([zeros, 2.0 * up_v[...].astype(F32)], axis=0).astype(BF)
    gq_ref[...] = jnp.zeros_like(gq_ref)
    gv_ref[...] = jnp.zeros_like(gv_ref)

    def flat(ref, cols=every):
        v = ref[:, :, :, :, :, cols]
        return v.reshape(-1, v.shape[-1])

    def thirds(fn):
        for n in range(3):
            fn(slice(HALF * n, HALF * (n + 1)))

    def each_row(fn, *args):
        def one(r, carry):
            fn(r, *args)
            return carry

        return lambda: lax.fori_loop(0, rows, one, 0)

    def each_half(fn, *args):
        def one(t, carry):
            fn(t // 2, pl.ds(pl.multiple_of(HALF * (t % 2), HALF), HALF), *args)
            return carry

        return lambda: lax.fori_loop(0, 2 * rows, one, 0)

    def turn(r):
        seg = jnp.broadcast_to(seg_ref[pl.ds(r, 1), :], (8, SEQ))
        perm_s[...] = turning(find_turn(seg))
        segb = seg.astype(F32).astype(BF)
        seg_row = dot_nt(perm_s[HALF:, :], segb)[:, 0:1]
        seg_col = dot_nt(segb, perm_s[HALF:, :])[0:1]
        bias = jnp.where(seg_col == seg_row, 0.0, -1e30)
        bias_s[r, :HALF] = bias
        bias_s[r, HALF:] = bias

        def part(c):
            x_s[r, :, c] = dot(perm_s[...], x_s[r, :, c]).astype(BF)
            g_s[r, :, c] = dot(perm_s[...], g_s[r, :, c]).astype(BF)

        thirds(part)

    def first_turn():
        for load in loads:
            load.wait()
        each_row(turn)()

    def project(r):
        low_s[r] = dot(x_s[r], flat(wq_s, slice(D, D + 2 * R))).astype(BF)

        def part(c):
            qkv_s[r, :, c] = (dot(x_s[r], flat(wq_s, c)) + dot(low_s[r], up_s[0, :, c])).astype(BF)

        thirds(part)

    def project_k(r):
        def part(c):
            qkv_s[r, :, D + c.start : D + c.stop] = dot(x_s[r], flat(wk_s, c)).astype(BF)

        thirds(part)

    def project_v(r):
        def part(c):
            v = dot(x_s[r], flat(wv_s, c)) + dot(low_s[r], up_s[1, :, c])
            qkv_s[r, :, 2 * D + c.start : 2 * D + c.stop] = v.astype(BF)

        thirds(part)

    def item(i, n):
        p, b = 2 * i + n // 2, n % 2
        return p, b, slice(HALF * b, HALF * (b + 1)), [pl.ds(pl.multiple_of(D * w + LANES * p, LANES), LANES) for w in range(3)]

    def heads(r):
        def some(i, carry):
            def scores(n, _):
                p, b, span, cut = item(i, n)
                s = dot_nt(two_heads(qkv_s[r, span, cut[0]] * 0.125), qkv_s[r, span, cut[1]])
                return s + bias_s[r] if b == 1 else s

            def soften(n, s):
                p, b, _, _ = item(i, n)
                e = jnp.exp(s - jnp.max(s, axis=1, keepdims=True))
                probs = (e * (1.0 / jnp.sum(e, axis=1, keepdims=True))).astype(BF)
                p_s[r, p, b] = probs
                return probs

            def context(n, probs):
                p, b, span, cut = item(i, n)
                ctx_s[r, span, cut[0]] = one_pair(dot(probs, qkv_s[r, span, cut[2]])).astype(BF)

            staged(4, scores, soften, context)
            return carry

        lax.fori_loop(0, PAIRS // 2, some, 0)

    def attended(r):
        z1 = x_s[r].astype(F32) + dot(ctx_s[r], flat(wo_s))
        z1 = z1 - mean(z1)
        r1 = lax.rsqrt(mean(z1 * z1) + 1e-5)
        n1 = z1 * r1
        n1_s[r] = n1
        r1_s[r] = r1
        hb_s[r] = (n1 * g1[...][None] + b1[...][None]).astype(BF)

    def inner(r, j):
        for n in range(3):
            c = slice(D * j + HALF * n, D * j + HALF * (n + 1))
            act, slope = gelu_parts(dot(hb_s[r], flat(win_s, c)))
            act_s[r, :, c] = act.astype(BF)
            gp_s[r, :, c] = slope.astype(BF)

    def outer(r, span, j):
        c = slice(HALF * j, HALF * (j + 1))
        return n1_s[r, span, c] * g1[...][None, c] + b1[...][None, c] + dot(act_s[r, span], flat(wout_s, c))

    def outer_first(r):
        dz_s[r, :, 0:HALF] = outer(r, slice(None), 0)

    def back(r):
        spans = [slice(HALF * b, HALF * (b + 1)) for b in range(2)]

        def summed(b, _):
            return [outer(r, spans[b], j) for j in (1, 2)]

        def second_norm(b, last):
            span = spans[b]
            z2 = jnp.concatenate([dz_s[r, span, 0:HALF], *last], axis=1)
            z2 = z2 - mean(z2)
            r2 = lax.rsqrt(mean(z2 * z2) + 1e-5)
            n2 = z2 * r2
            out_s[r, span] = (n2 * g2[...][None] + b2[...][None]).astype(BF)
            pltpu.make_async_copy(out_s.at[r, span], y_hbm.at[r, span], iosem.at[3]).start()
            dn2 = g_s[r, span].astype(F32) * g2[...][None]
            dz2 = r2 * (dn2 - mean(dn2) - n2 * mean(dn2 * n2))
            dz_s[r, span] = dz2
            return dz2.astype(BF)

        def inner_back(b, df):
            for n in range(4):
                c = slice(D * n, D * (n + 1))
                dact = dot_nt(df, wout_s[n].reshape(D, D))
                act_s[r, spans[b], c] = (dact * gp_s[r, spans[b], c].astype(F32)).astype(BF)

        def hidden_back(b, _):
            return dot_nt(act_s[r, spans[b]], flat(win_s))

        def first_norm(b, dh):
            span = spans[b]
            dn1 = (dz_s[r, span] + dh) * g1[...][None]
            n1 = n1_s[r, span]
            dz1 = r1_s[r, span] * (dn1 - mean(dn1) - n1 * mean(dn1 * n1))
            dz_s[r, span] = dz1
            return dz1.astype(BF)

        def context_back(b, dz1):
            ctx_s[r, spans[b]] = dot_nt(dz1, flat(wo_s)).astype(BF)

        staged(2, summed, second_norm, inner_back, hidden_back, first_norm, context_back)

    def heads_back(t, carry):
        r, i = t // (PAIRS // 2), t % (PAIRS // 2)

        def to(n):
            return slice(HALF * (n % 2), HALF * (n % 2 + 1)), slice(LANES * (n // 2), LANES * (n // 2 + 1))

        def values(n, _):
            p, b, span, cut = item(i, n)
            dc = two_heads(ctx_s[r, span, cut[0]])
            dp = dot_nt(dc, qkv_s[r, span, cut[2]])
            two_s[2, *to(n)] = dot_tn(dc, p_s[r, p, b]).T.astype(BF)
            return dp

        def scores(n, dp):
            p, b, _, _ = item(i, n)
            probs = p_s[r, p, b].astype(F32)
            return (probs * (dp - jnp.sum(probs * dp, axis=1, keepdims=True))).astype(BF)

        def sides(n, ds):
            p, b, span, cut = item(i, n)
            q, k = qkv_s[r, span, cut[0]], qkv_s[r, span, cut[1]]
            two_s[0, *to(n)] = (one_pair(dot(ds, k)) * 0.125).astype(BF)
            two_s[1, *to(n)] = dot_tn(two_heads(q * 0.125), ds).T.astype(BF)

        staged(4, values, scores, sides)
        for w in range(3):
            qkv_s[r, :, pl.ds(pl.multiple_of(D * w + 2 * LANES * i, LANES), 2 * LANES)] = two_s[w]
        return carry

    def grads(r):
        gq_ref[...] += 2.0 * dot_tn(low_s[r], qkv_s[r, :, :D])[:R]
        gv_ref[...] += 2.0 * dot_tn(low_s[r], qkv_s[r, :, 2 * D :])[R:]

    def tokens_back(r, span):
        dq, dk, dv = (qkv_s[r, span, D * w : D * (w + 1)] for w in range(3))
        dlow = (dot_nt(dq, up_s[0]) + dot_nt(dv, up_s[1])).astype(BF)
        tg = dz_s[r, span] + dot_nt(dq, flat(wq_s, slice(0, D))) + dot_nt(dk, flat(wk_s)) + dot_nt(dv, flat(wv_s))
        out_s[r, span] = (tg + dot_nt(dlow, flat(wq_s, slice(D, D + 2 * R)))).astype(BF)
        pltpu.make_async_copy(out_s.at[r, span], tg_hbm.at[r, span], iosem.at[4]).start()

    works = [
        (set(), first_turn),
        ({wq_g}, each_row(project)),
        ({wk_g}, each_row(project_k)),
        ({wv_g}, each_row(project_v)),
    ]
    works += [({wv_g}, functools.partial(heads, r)) for r in range(rows)]
    works += [({wo_g}, each_row(attended))]
    works += [({win_g + j}, functools.partial(inner, r, j)) for j in range(4) for r in range(rows)]
    works += [({wout_g}, each_row(outer_first))]
    net.run(works)
    net.need(wout_g + 1, wout_g + 2)
    each_row(back)()
    lax.fori_loop(0, rows * PAIRS // 2, heads_back, 0)
    each_row(grads)()
    pltpu.make_async_copy(out_s, y_hbm, iosem.at[3]).wait()
    if remote:
        sums = Sums(net, gq_ref, gv_ref, mine_s, plane_s, line_s, ssem2, rsem2)
        sums.over_plane()

        def last(r, span):
            tokens_back(r, span)
            pl.when((r == 0) & (span.start > 0))(sums.over_line)

        each_half(last)()
        net.drain()
        sums.finish()
    else:
        each_half(tokens_back)()
    pltpu.make_async_copy(out_s, tg_hbm, iosem.at[4]).wait()


def unturn_kernel(seg_ref, y_ref, tg_ref, gq_ref, gv_ref, oy_ref, otg_ref, oq_ref, ov_ref, perm_s):
    perm_s[...] = turning(-find_turn(jnp.broadcast_to(seg_ref[pl.ds(pl.program_id(0), 1), :], (8, SEQ))))
    oy_ref[0] = dot(perm_s[...], y_ref[0]).astype(BF)
    otg_ref[0] = dot(perm_s[...], tg_ref[0]).astype(BF)
    oq_ref[...] = gq_ref[...]
    ov_ref[...] = gv_ref[...]


def unturn(seg, y, tg, gq, gv):
    def whole(v):
        return pl.BlockSpec(v.shape, lambda r: (0, 0))

    part = pl.BlockSpec((1, SEQ, D), lambda r: (r, 0, 0))
    act, grad = jax.ShapeDtypeStruct(y.shape, BF), jax.ShapeDtypeStruct(gq.shape, F32)
    return pl.pallas_call(
        unturn_kernel,
        grid=(y.shape[0],),
        out_shape=[act, act, grad, grad],
        in_specs=[whole(seg), part, part, whole(gq), whole(gv)],
        out_specs=[part, part, whole(gq), whole(gv)],
        scratch_shapes=[pltpu.VMEM((SEQ, SEQ), BF)],
        name="unturn",
    )(seg, y, tg, gq, gv)


def run_layer(remote, seg, x, g, mats, downs, ups, norms):
    rows = x.shape[0]
    vmem, hbm = pl.BlockSpec(memory_space=pltpu.VMEM), pl.BlockSpec(memory_space=pl.ANY)
    act, grad = jax.ShapeDtypeStruct(x.shape, BF), jax.ShapeDtypeStruct((R, D), F32)
    blocks = 11
    shapes = [
        ((4, 4, 2, 3, 8, WIDE), BF),
        ((4, 4, 2, 3, 8, D), BF),
        ((4, 4, 2, 3, 8, D), BF),
        ((4, 4, 2, 3, 8, D), BF),
        ((4, 4, 2, 3, 8, FF), BF),
        ((4, 4, 2, 12, 8, D), BF),
        ((3, 8, WIDE), BF),
        ((LANES, LANES), F32),
        ((2, 2 * R, D), BF),
        ((rows, SEQ, D), BF),
        ((rows, SEQ, D), BF),
        ((SEQ, SEQ), BF),
        ((rows, SEQ, HALF), F32),
        ((rows, SEQ, 2 * R), BF),
        ((rows, SEQ, 3 * D), BF),
        ((rows, PAIRS, 2, SEQ, HALF), BF),
        ((rows, SEQ, D), BF),
        ((rows, SEQ, D), F32),
        ((rows, SEQ, 1), F32),
        ((rows, SEQ, D), BF),
        ((rows, SEQ, FF), BF),
        ((rows, SEQ, FF), BF),
        ((rows, SEQ, D), F32),
        ((rows, SEQ, D), BF),
        ((3, SEQ, 2 * LANES), BF),
    ]
    dma = pltpu.SemaphoreType.DMA
    return pl.pallas_call(
        functools.partial(layer_kernel, remote),
        out_shape=[act, act, grad, grad],
        in_specs=[vmem] * 9 + [hbm] * 8,
        out_specs=[hbm, hbm, vmem, vmem],
        scratch_shapes=[pltpu.VMEM(*s) for s in shapes]
        + [dma((blocks,)), dma((blocks, 11)), dma((blocks,)), dma((5,))]
        + [pltpu.VMEM((n, R, D), F32) for n in (2, 8)] + [pltpu.VMEM((2, 4, R, D), F32), dma((14,)), dma((14,))],
        compiler_params=pltpu.CompilerParams(
            vmem_limit_bytes=64 << 20,
            **({"collective_id": 0, "has_side_effects": True} if remote else {}),
        ),
        name="layer",
    )(seg, *ups, *norms, *downs, x, g, *mats)


def solution(mesh):
    remote = dict(mesh.shape) == {"dp": 8, "fsdp": 4}

    def body(
        tokens, segments, w_query, w_key, w_value, w_output, w_inner, w_outer, down_query, down_value,
        up_query, up_value, norm1_gain, norm1_shift, norm2_gain, norm2_shift, out_grad,
    ):
        mats = [w_query, w_key, w_value, w_output, w_inner, w_outer]
        if remote:
            mats = [m.reshape(-1, 8, m.shape[1]) for m in mats]
        else:
            pad = jnp.zeros((w_query.shape[0], LANES - 2 * R), BF)
            mats[0] = jnp.concatenate([w_query, down_query, down_value, pad], axis=1)
            mats = [lax.all_gather(m, AXES, axis=0, tiled=True) for m in mats]
            mats = [m.reshape(4, 4, 2, -1, 8, m.shape[1]) for m in mats]
        y, tg, gq, gv = run_layer(
            remote,
            segments,
            tokens,
            out_grad,
            mats,
            (down_query.T, down_value.T),
            (up_query, up_value),
            (norm1_gain, norm1_shift, norm2_gain, norm2_shift),
        )
        if not remote:
            gq, gv = lax.psum((gq, gv), AXES)
        return unturn(segments, y, tg, gq, gv)

    split, copied = P(AXES), P()
    return jax.shard_map(
        body,
        mesh=mesh,
        in_specs=(split,) * 10 + (copied,) * 6 + (split,),
        out_specs=(split, split, copied, copied),
        check_vma=False,
    )
```

```python
import functools

import jax
import jax.numpy as jnp
from jax import lax
from jax.experimental import pallas as pl
from jax.experimental.pallas import tpu as pltpu
from jax.sharding import PartitionSpec as P

MESH = pl.DeviceIdType.MESH
D, H, HD, FF, R, SEQ = 768, 12, 64, 3072, 8, 512
HALF, PAIRS, LANES = SEQ // 2, H // 2, 128
WIDE = D + LANES
BF, F32 = jnp.bfloat16, jnp.float32
AXES = ("dp", "fsdp")


def dot(a, b):
    return lax.dot_general(a, b, (((1,), (0,)), ((), ())), preferred_element_type=F32)


def dot_nt(a, b):
    return lax.dot_general(a, b, (((1,), (1,)), ((), ())), preferred_element_type=F32)


def dot_tn(a, b):
    return lax.dot_general(a, b, (((0,), (0,)), ((), ())), preferred_element_type=F32)


def mean(v):
    return jnp.mean(v, axis=-1, keepdims=True)


def gelu_parts(u):
    dens = jnp.exp2(u * u * -0.7213475204444817)
    t = 1.0 / (jnp.abs(u) * (0.3275911 * 0.7071067811865476) + 1.0)
    poly = (((0.5307027145 * t - 0.7265760135) * t + 0.7107068705) * t - 0.142248368) * t + 0.127414796
    tail = poly * t * dens
    phi = jnp.where(u < 0, tail, 1.0 - tail)
    return u * phi, phi + u * dens * 0.3989422804014327


def two_heads(v):
    first = lax.broadcasted_iota(jnp.int32, v.shape, 1) < HD
    zero = jnp.zeros_like(v)
    return jnp.concatenate([jnp.where(first, v, zero), jnp.where(first, zero, v)], axis=0)


def one_pair(v):
    first = lax.broadcasted_iota(jnp.int32, (HALF, 2 * HD), 1) < HD
    return jnp.where(first, v[:HALF], v[HALF:])


def staged(count, *stages):
    held = [None] * count
    for t in range(count + len(stages) - 1):
        for k, stage in enumerate(stages):
            if 0 <= t - k < count:
                held[t - k] = stage(t - k, held[t - k])


class Links:
    def __init__(self, groups, flat, early, ssem, rsem, lsem):
        self.early = early
        self.groups, self.flat, self.ssem, self.rsem, self.lsem = groups, flat, ssem, rsem, lsem
        dp, fs = lax.axis_index("dp"), lax.axis_index("fsdp")
        z, x, y, c = self.z, self.x, self.y, self.c = dp // 2, dp % 2, fs // 2, fs % 2
        xa, ya = jnp.where(c == 0, x, 1 - x), jnp.where(c == 0, 1 - y, y)
        xb, yb = jnp.where(c == 0, 1 - x, x), jnp.where(c == 0, y, 1 - y)
        self.near, self.far = self.device(z, xa, ya, c), self.device(z, xb, yb, c)
        self.twin, self.diag = self.device(z, x, y, 1 - c), self.device(z, 1 - x, 1 - y, c)
        self.line = [self.device((z + d) % 4, x, y, c) for d in (1, 2, 3)]
        self.up, self.down = self.device(jnp.minimum(z + 1, 3), x, y, c), self.device(jnp.maximum(z - 1, 0), x, y, c)
        self.mine, self.at_near, self.at_far, self.at_diag = x * 2 + y, xa * 2 + ya, xb * 2 + yb, 3 - x * 2 - y

    @staticmethod
    def device(z, x, y, c):
        return (z * 2 + x, y * 2 + c)

    def meet(self):
        barrier = pltpu.get_barrier_semaphore()
        others = [to for _, to in self.in_plane()] + self.on_line()[1:]
        for other in others:
            pl.semaphore_signal(barrier, 1, device_id=other, device_id_type=MESH)
        pl.semaphore_wait(barrier, len(others))

    def in_plane(self):
        there = [(n // 4, n // 2 % 2, n % 2) for n in range(1, 8)]
        place = [((self.x + i) % 2, (self.y + j) % 2, (self.c + k) % 2) for i, j, k in there]
        return [(c, self.device(self.z, x, y, c)) for x, y, c in place]

    def on_line(self):
        there = [(0, 1)] + [(d, k) for d in (1, 2, 3) for k in (0, 1)]
        return [self.device((self.z + d) % 4, self.x, self.y, (self.c + k) % 2) for d, k in there]

    def at_column(self, g, chip):
        _, buf, cols = self.groups[g]
        return buf.at[:, chip, self.c, :, :, cols]

    def at_plane(self, g, z):
        _, buf, cols = self.groups[g]
        return buf.at[z, :, self.c, :, :, cols]

    def at_piece(self, g, chip):
        _, buf, cols = self.groups[g]
        return buf.at[self.z, chip, self.c, :, :, cols]

    def send(self, g, src, dst, k, to):
        pltpu.make_async_remote_copy(
            src_ref=src,
            dst_ref=dst,
            send_sem=self.ssem.at[g],
            recv_sem=self.rsem.at[g, k],
            device_id=to,
            device_id_type=MESH,
        ).start()

    @staticmethod
    def wait(ref, sem):
        pltpu.make_async_copy(ref, ref, sem).wait()


    def own(self, g):
        src = self.groups[g][0]
        pltpu.make_async_copy(src, self.at_piece(g, self.mine), self.lsem.at[g]).start()
        for d in range(3):
            self.send(g, src, self.at_piece(g, self.mine), d, self.line[d])
        if g in self.early:
            self.send(g, src, self.at_piece(g, self.mine), 3, self.near)
            self.send(g, src, self.at_piece(g, self.mine), 4, self.far)

    def column_on(self, g, chip, *to):
        for k, other in to:
            self.send(g, self.at_column(g, chip), self.at_column(g, chip), k, other)

    def after_line(self, g):
        src = self.groups[g][0]
        self.wait(src, self.lsem.at[g])
        for d in range(3):
            self.wait(src, self.rsem.at[g, d])
        if g in self.early:
            _, buf, cols = self.groups[g]
            for k, other in ((3, self.near), (4, self.far)):
                for d in (1, 2, 3):
                    piece = buf.at[(self.z + d) % 4, self.mine, self.c, :, :, cols]
                    self.send(g, piece, piece, k, other)
            self.column_on(g, self.mine, (6, self.twin))
        else:
            self.column_on(g, self.mine, (3, self.near), (4, self.far), (6, self.twin))

    def after_near(self, g):
        self.wait(self.at_column(g, self.at_near), self.rsem.at[g, 3])
        self.column_on(g, self.at_near, (5, self.far), (7, self.twin))

    def after_far(self, g):
        self.wait(self.at_column(g, self.at_far), self.rsem.at[g, 4])
        self.column_on(g, self.at_far, (8, self.twin))

    def after_diag(self, g):
        self.wait(self.at_column(g, self.at_diag), self.rsem.at[g, 5])
        self.column_on(g, self.at_diag, (9, self.twin))

    def whole(self, g):
        for k in range(4):
            self.wait(self.at_column(g, self.mine), self.rsem.at[g, 6 + k])


    def own_flat(self, g):
        src = self.groups[g][0]
        pltpu.make_async_copy(src, self.at_piece(g, self.mine), self.lsem.at[g]).start()
        self.send(g, src, self.at_piece(g, self.mine), 0, self.near)
        self.send(g, src, self.at_piece(g, self.mine), 1, self.far)

    def near_flat(self, g):
        piece = self.at_piece(g, self.at_near)
        self.wait(piece, self.rsem.at[g, 0])
        self.send(g, piece, piece, 2, self.far)

    def plane_on(self, g, z, up, down):
        plane = self.at_plane(g, z)
        if up:
            pl.when(self.z < 3)(lambda: self.send(g, plane, plane, 3 + z, self.up))
        if down:
            pl.when(self.z > 0)(lambda: self.send(g, plane, plane, 3 + z, self.down))
        self.send(g, plane, plane, 7 + z, self.twin)

    def plane_flat(self, g):
        src = self.groups[g][0]
        self.wait(src, self.lsem.at[g])
        self.wait(src, self.rsem.at[g, 1])
        self.wait(src, self.rsem.at[g, 2])
        self.plane_on(g, self.z, True, True)

    def hop_flat(self, d, g):
        def below():
            self.wait(self.at_plane(g, self.z - d), self.rsem.at[g, 3 + self.z - d])
            self.plane_on(g, self.z - d, True, False)

        def above():
            self.wait(self.at_plane(g, self.z + d), self.rsem.at[g, 3 + self.z + d])
            self.plane_on(g, self.z + d, False, True)

        pl.when(self.z >= d)(below)
        pl.when(self.z + d <= 3)(above)

    def whole_flat(self, g):
        for z in range(4):
            self.wait(self.at_plane(g, z), self.rsem.at[g, 7 + z])

    def plan(self):
        first = [g for g in range(len(self.groups)) if g not in self.flat]
        steps = [(self.own, g) for g in first] + [(self.own_flat, g) for g in self.flat]
        stages = (self.after_line, self.after_near, self.after_far, self.after_diag, self.whole)
        main = []
        for t in range(len(first) + len(stages) - 1):
            for k, stage in enumerate(stages):
                if 0 <= t - k < len(first):
                    main.append((stage, first[t - k]))
        side = [self.near_flat, self.plane_flat] + [functools.partial(self.hop_flat, d) for d in (1, 2, 3)]
        when = ((0.12, 0.14), (0.25, 0.30), (0.45, 0.55), (0.65, 0.75), (0.85, 0.95))
        extra = [(f, (stage, g)) for stage, fs in zip(side, when) for f, g in zip(fs, self.flat)]
        for f, item in sorted(extra, key=lambda e: -e[0]):
            main.insert(int(f * len(main)), item)
        return steps, main + [(self.whole_flat, g) for g in self.flat]

    def run(self, works):
        steps, main = self.plan()
        for step, g in steps:
            step(g)
        ends = (self.whole, self.whole_flat)
        here, todo = set(), list(works)
        for step, g in main:
            if todo and todo[0][0] <= here:
                todo.pop(0)[1]()
            step(g)
            if step in ends:
                here.add(g)
        for _, fn in todo:
            fn()

    def need(self, *groups):
        pass

    def drain(self):
        for g, (src, _, _) in enumerate(self.groups):
            for _ in range(3):
                self.wait(src, self.ssem.at[g])
            if g in self.flat:
                plane = self.at_plane(g, 0)
                sent = 4 + jnp.where(self.z < 3, self.z + 1, 0) + jnp.where(self.z > 0, 4 - self.z, 0)
                lax.fori_loop(0, sent, lambda _, v: (self.wait(plane, self.ssem.at[g]), v)[1], 0)
            else:
                for _ in range(7):
                    self.wait(self.at_column(g, self.mine), self.ssem.at[g])


class Local:
    def __init__(self, groups, lsem):
        self.copies = [
            pltpu.make_async_copy(src, buf.at[:, :, :, :, :, cols], lsem.at[g]) for g, (src, buf, cols) in enumerate(groups)
        ]

    def run(self, works):
        for copy in self.copies:
            copy.start()
        here = set()
        for needs, fn in works:
            for g in sorted(needs - here):
                self.copies[g].wait()
            here |= needs
            fn()

    def need(self, *groups):
        for g in groups:
            self.copies[g].wait()

    def drain(self):
        pass


class Sums:
    def __init__(self, links, q, v, mine, plane, line, ssem, rsem):
        self.k, self.q, self.v, self.mine, self.plane, self.line = links, q, v, mine, plane, line
        self.ssem, self.rsem, self.sends = ssem, rsem, []

    def copy(self, ref, to_ref, k, to):
        send = pltpu.make_async_remote_copy(
            src_ref=ref,
            dst_ref=to_ref,
            send_sem=self.ssem.at[k],
            recv_sem=self.rsem.at[k],
            device_id=to,
            device_id_type=MESH,
        )
        send.start()
        self.sends.append(send)

    def over_plane(self):
        k = self.k
        slot = self.plane.at[(k.x * 2 + k.y) * 2 + k.c]
        self.mine[0], self.mine[1] = self.q[...], self.v[...]
        self.plane[(k.x * 2 + k.y) * 2 + k.c] = self.mine[k.c]
        for n, (core, to) in enumerate(k.in_plane()):
            self.copy(self.mine.at[core], slot, n, to)

    def end(self):
        for s in self.sends:
            s.wait()
        self.sends = []

    def over_line(self):
        self.end()
        k, p = self.k, self.plane
        self.line[k.c, k.z] = ((p[0] + p[1]) + (p[2] + p[3])) + ((p[4] + p[5]) + (p[6] + p[7]))
        places = self.line.at[k.c, k.z]
        for n, to in enumerate(k.on_line()):
            self.copy(places, places, 7 + n, to)

    def finish(self):
        p = self.line
        for n in range(7):
            pltpu.make_async_copy(p.at[0, 0], p.at[0, 0], self.rsem.at[7 + n]).wait()
            pltpu.make_async_copy(p.at[0, 0], p.at[0, 0], self.ssem.at[7 + n]).wait()
        self.q[...] = (p[0, 0] + p[0, 1]) + (p[0, 2] + p[0, 3])
        self.v[...] = (p[1, 0] + p[1, 1]) + (p[1, 2] + p[1, 3])


def find_turn(seg):
    lane = lax.broadcasted_iota(jnp.int32, (8, SEQ), 1)
    hit = (seg == pltpu.roll(seg, SEQ - HALF + 1, 1)) & (lane <= HALF)
    return jnp.min(jnp.where(hit, lane, SEQ), axis=1, keepdims=True)[0:1]


def turning(by):
    i = lax.broadcasted_iota(jnp.int32, (SEQ, SEQ), 0)
    diff = lax.broadcasted_iota(jnp.int32, (SEQ, SEQ), 1) - i - by
    return jnp.where((diff == 0) | (diff == SEQ) | (diff == -SEQ), 1.0, 0.0).astype(BF)


def layer_kernel(
    remote,
    seg_ref, up_q, up_v, g1, b1, g2, b2, dqt, dvt, x_hbm, g_hbm, wq_h, wk_h, wv_h, wo_h, win_h, wout_h,
    y_hbm, tg_hbm, gq_ref, gv_ref,
    wq_s, wk_s, wv_s, wo_s, win_s, wout_s, own_s, flip_s, up_s,
    x_s, g_s, perm_s, bias_s, low_s, qkv_s, p_s, ctx_s, n1_s, r1_s, hb_s, act_s, gp_s, dz_s, out_s, two_s,
    ssem, rsem, lsem, iosem, mine_s, plane_s, line_s, ssem2, rsem2,
):
    rows = x_s.shape[0]
    loads = [pltpu.make_async_copy(src, dst, iosem.at[k]) for k, (src, dst) in enumerate(((x_hbm, x_s), (g_hbm, g_s)))]
    for load in loads:
        load.start()

    every, col = slice(None), pl.ds
    groups = [(own_s if remote else wq_h, wq_s, every), (wk_h, wk_s, every), (wv_h, wv_s, every), (wo_h, wo_s, every)]
    lead = (every,) * (2 if remote else 5)
    groups += [(win_h.at[(*lead, col(D * j, D))], win_s, col(D * j, D)) for j in range(4)]
    groups += [(wout_h.at[(*lead, col(HALF * j, HALF))], wout_s, col(HALF * j, HALF)) for j in range(3)]
    wq_g, wk_g, wv_g, wo_g, win_g, wout_g = 0, 1, 2, 3, 4, 8

    if remote:
        stage = pltpu.make_async_copy(wq_h, own_s.at[:, :, col(0, D)], iosem.at[2])
        stage.start()
        flip_s[...] = jnp.zeros_like(flip_s)
        flip_s[0:R, 0 : dqt.shape[1]] = dqt[...].astype(F32)
        flip_s[R : 2 * R, 0 : dvt.shape[1]] = dvt[...].astype(F32)
        downs = flip_s[...].T[0 : dqt.shape[1]].astype(BF)
        own_s[:, :, D:] = downs.reshape(*own_s.shape[:2], LANES)
        net = Links(groups, (wout_g + 1, wout_g + 2), (0, 1, 2, 3, 4), ssem, rsem, lsem)
        net.meet()
        stage.wait()
    else:
        net = Local(groups, lsem)
    zeros = jnp.zeros((R, D), F32)
    up_s[0] = jnp.concatenate([2.0 * up_q[...].astype(F32), zeros], axis=0).astype(BF)
    up_s[1] = jnp.concatenate([zeros, 2.0 * up_v[...].astype(F32)], axis=0).astype(BF)
    gq_ref[...] = jnp.zeros_like(gq_ref)
    gv_ref[...] = jnp.zeros_like(gv_ref)

    def flat(ref, cols=every):
        v = ref[:, :, :, :, :, cols]
        return v.reshape(-1, v.shape[-1])

    def thirds(fn):
        for n in range(3):
            fn(slice(HALF * n, HALF * (n + 1)))

    def each_row(fn, *args):
        def one(r, carry):
            fn(r, *args)
            return carry

        return lambda: lax.fori_loop(0, rows, one, 0)

    def each_half(fn, *args):
        def one(t, carry):
            fn(t // 2, pl.ds(pl.multiple_of(HALF * (t % 2), HALF), HALF), *args)
            return carry

        return lambda: lax.fori_loop(0, 2 * rows, one, 0)

    def turn(r):
        seg = jnp.broadcast_to(seg_ref[pl.ds(r, 1), :], (8, SEQ))
        perm_s[...] = turning(find_turn(seg))
        segb = seg.astype(F32).astype(BF)
        seg_row = dot_nt(perm_s[HALF:, :], segb)[:, 0:1]
        seg_col = dot_nt(segb, perm_s[HALF:, :])[0:1]
        bias = jnp.where(seg_col == seg_row, 0.0, -1e30)
        bias_s[r, :HALF] = bias
        bias_s[r, HALF:] = bias

        def part(c):
            x_s[r, :, c] = dot(perm_s[...], x_s[r, :, c]).astype(BF)
            g_s[r, :, c] = dot(perm_s[...], g_s[r, :, c]).astype(BF)

        thirds(part)

    def first_turn():
        for load in loads:
            load.wait()
        each_row(turn)()

    def project(r):
        low_s[r] = dot(x_s[r], flat(wq_s, slice(D, D + 2 * R))).astype(BF)

        def part(c):
            qkv_s[r, :, c] = (dot(x_s[r], flat(wq_s, c)) + dot(low_s[r], up_s[0, :, c])).astype(BF)

        thirds(part)

    def project_k(r):
        def part(c):
            qkv_s[r, :, D + c.start : D + c.stop] = dot(x_s[r], flat(wk_s, c)).astype(BF)

        thirds(part)

    def project_v(r):
        def part(c):
            v = dot(x_s[r], flat(wv_s, c)) + dot(low_s[r], up_s[1, :, c])
            qkv_s[r, :, 2 * D + c.start : 2 * D + c.stop] = v.astype(BF)

        thirds(part)

    def item(i, n):
        p, b = 2 * i + n // 2, n % 2
        return p, b, slice(HALF * b, HALF * (b + 1)), [pl.ds(pl.multiple_of(D * w + LANES * p, LANES), LANES) for w in range(3)]

    def heads(r):
        def some(i, carry):
            def scores(n, _):
                p, b, span, cut = item(i, n)
                s = dot_nt(two_heads(qkv_s[r, span, cut[0]] * 0.125), qkv_s[r, span, cut[1]])
                return s + bias_s[r] if b == 1 else s

            def soften(n, s):
                p, b, _, _ = item(i, n)
                e = jnp.exp(s - jnp.max(s, axis=1, keepdims=True))
                probs = (e * (1.0 / jnp.sum(e, axis=1, keepdims=True))).astype(BF)
                p_s[r, p, b] = probs
                return probs

            def context(n, probs):
                p, b, span, cut = item(i, n)
                ctx_s[r, span, cut[0]] = one_pair(dot(probs, qkv_s[r, span, cut[2]])).astype(BF)

            staged(4, scores, soften, context)
            return carry

        lax.fori_loop(0, PAIRS // 2, some, 0)

    def attended(r):
        z1 = x_s[r].astype(F32) + dot(ctx_s[r], flat(wo_s))
        z1 = z1 - mean(z1)
        r1 = lax.rsqrt(mean(z1 * z1) + 1e-5)
        n1 = z1 * r1
        n1_s[r] = n1
        r1_s[r] = r1
        hb_s[r] = (n1 * g1[...][None] + b1[...][None]).astype(BF)

    def inner(r, j):
        for n in range(3):
            c = slice(D * j + HALF * n, D * j + HALF * (n + 1))
            act, slope = gelu_parts(dot(hb_s[r], flat(win_s, c)))
            act_s[r, :, c] = act.astype(BF)
            gp_s[r, :, c] = slope.astype(BF)

    def outer(r, span, j):
        c = slice(HALF * j, HALF * (j + 1))
        return n1_s[r, span, c] * g1[...][None, c] + b1[...][None, c] + dot(act_s[r, span], flat(wout_s, c))

    def outer_first(r):
        dz_s[r, :, 0:HALF] = outer(r, slice(None), 0)

    def back(r):
        spans = [slice(HALF * b, HALF * (b + 1)) for b in range(2)]

        def summed(b, _):
            return [outer(r, spans[b], j) for j in (1, 2)]

        def second_norm(b, last):
            span = spans[b]
            z2 = jnp.concatenate([dz_s[r, span, 0:HALF], *last], axis=1)
            z2 = z2 - mean(z2)
            r2 = lax.rsqrt(mean(z2 * z2) + 1e-5)
            n2 = z2 * r2
            out_s[r, span] = (n2 * g2[...][None] + b2[...][None]).astype(BF)
            pltpu.make_async_copy(out_s.at[r, span], y_hbm.at[r, span], iosem.at[3]).start()
            dn2 = g_s[r, span].astype(F32) * g2[...][None]
            dz2 = r2 * (dn2 - mean(dn2) - n2 * mean(dn2 * n2))
            dz_s[r, span] = dz2
            return dz2.astype(BF)

        def inner_back(b, df):
            for n in range(4):
                c = slice(D * n, D * (n + 1))
                dact = dot_nt(df, wout_s[n].reshape(D, D))
                act_s[r, spans[b], c] = (dact * gp_s[r, spans[b], c].astype(F32)).astype(BF)

        def hidden_back(b, _):
            return dot_nt(act_s[r, spans[b]], flat(win_s))

        def first_norm(b, dh):
            span = spans[b]
            dn1 = (dz_s[r, span] + dh) * g1[...][None]
            n1 = n1_s[r, span]
            dz1 = r1_s[r, span] * (dn1 - mean(dn1) - n1 * mean(dn1 * n1))
            dz_s[r, span] = dz1
            return dz1.astype(BF)

        def context_back(b, dz1):
            ctx_s[r, spans[b]] = dot_nt(dz1, flat(wo_s)).astype(BF)

        staged(2, summed, second_norm, inner_back, hidden_back, first_norm, context_back)

    def heads_back(t, carry):
        r, i = t // (PAIRS // 2), t % (PAIRS // 2)

        def to(n):
            return slice(HALF * (n % 2), HALF * (n % 2 + 1)), slice(LANES * (n // 2), LANES * (n // 2 + 1))

        def values(n, _):
            p, b, span, cut = item(i, n)
            dc = two_heads(ctx_s[r, span, cut[0]])
            dp = dot_nt(dc, qkv_s[r, span, cut[2]])
            two_s[2, *to(n)] = dot_tn(dc, p_s[r, p, b]).T.astype(BF)
            return dp

        def scores(n, dp):
            p, b, _, _ = item(i, n)
            probs = p_s[r, p, b].astype(F32)
            return (probs * (dp - jnp.sum(probs * dp, axis=1, keepdims=True))).astype(BF)

        def sides(n, ds):
            p, b, span, cut = item(i, n)
            two_s[0, *to(n)] = (one_pair(dot(ds, qkv_s[r, span, cut[1]])) * 0.125).astype(BF)
            p_s[r, p, b] = ds

        staged(4, values, scores, sides)
        hb_s[r, :, pl.ds(pl.multiple_of(2 * LANES * i, LANES), 2 * LANES)] = two_s[0]
        qkv_s[r, :, pl.ds(pl.multiple_of(2 * D + 2 * LANES * i, LANES), 2 * LANES)] = two_s[2]
        return carry

    def keys_back(t, carry):
        r, i = t // (PAIRS // 2), t % (PAIRS // 2)
        for n in range(4):
            p, b, span, cut = item(i, n)
            dk = dot_tn(two_heads(qkv_s[r, span, cut[0]] * 0.125), p_s[r, p, b]).T.astype(BF)
            two_s[1, span, LANES * (n // 2) : LANES * (n // 2 + 1)] = dk
        qkv_s[r, :, pl.ds(pl.multiple_of(D + 2 * LANES * i, LANES), 2 * LANES)] = two_s[1]
        return carry

    def grads(r):
        gq_ref[...] += 2.0 * dot_tn(low_s[r], hb_s[r])[:R]
        gv_ref[...] += 2.0 * dot_tn(low_s[r], qkv_s[r, :, 2 * D :])[R:]

    def tokens_back(r, span):
        dq, dk, dv = hb_s[r, span], qkv_s[r, span, D : 2 * D], qkv_s[r, span, 2 * D :]
        dlow = (dot_nt(dq, up_s[0]) + dot_nt(dv, up_s[1])).astype(BF)
        tg = dz_s[r, span] + dot_nt(dq, flat(wq_s, slice(0, D))) + dot_nt(dk, flat(wk_s)) + dot_nt(dv, flat(wv_s))
        out_s[r, span] = (tg + dot_nt(dlow, flat(wq_s, slice(D, D + 2 * R)))).astype(BF)
        pltpu.make_async_copy(out_s.at[r, span], tg_hbm.at[r, span], iosem.at[4]).start()

    works = [
        (set(), first_turn),
        ({wq_g}, each_row(project)),
        ({wk_g}, each_row(project_k)),
        ({wv_g}, each_row(project_v)),
    ]
    works += [({wv_g}, functools.partial(heads, r)) for r in range(rows)]
    works += [({wo_g}, each_row(attended))]
    works += [({win_g + j}, functools.partial(inner, r, j)) for j in range(4) for r in range(rows)]
    works += [({wout_g}, each_row(outer_first))]
    net.run(works)
    net.need(wout_g + 1, wout_g + 2)
    each_row(back)()
    lax.fori_loop(0, rows * PAIRS // 2, heads_back, 0)
    each_row(grads)()
    pltpu.make_async_copy(out_s, y_hbm, iosem.at[3]).wait()
    if remote:
        sums = Sums(net, gq_ref, gv_ref, mine_s, plane_s, line_s, ssem2, rsem2)
        sums.over_plane()
        lax.fori_loop(0, rows * PAIRS // 2, keys_back, 0)
        sums.over_line()
        each_half(tokens_back)()
        net.drain()
        sums.finish()
    else:
        lax.fori_loop(0, rows * PAIRS // 2, keys_back, 0)
        each_half(tokens_back)()
    pltpu.make_async_copy(out_s, tg_hbm, iosem.at[4]).wait()


def unturn_kernel(seg_ref, y_ref, tg_ref, gq_ref, gv_ref, oy_ref, otg_ref, oq_ref, ov_ref, perm_s):
    perm_s[...] = turning(-find_turn(jnp.broadcast_to(seg_ref[pl.ds(pl.program_id(0), 1), :], (8, SEQ))))
    oy_ref[0] = dot(perm_s[...], y_ref[0]).astype(BF)
    otg_ref[0] = dot(perm_s[...], tg_ref[0]).astype(BF)
    oq_ref[...] = gq_ref[...]
    ov_ref[...] = gv_ref[...]


def unturn(seg, y, tg, gq, gv):
    def whole(v):
        return pl.BlockSpec(v.shape, lambda r: (0, 0))

    part = pl.BlockSpec((1, SEQ, D), lambda r: (r, 0, 0))
    act, grad = jax.ShapeDtypeStruct(y.shape, BF), jax.ShapeDtypeStruct(gq.shape, F32)
    return pl.pallas_call(
        unturn_kernel,
        grid=(y.shape[0],),
        out_shape=[act, act, grad, grad],
        in_specs=[whole(seg), part, part, whole(gq), whole(gv)],
        out_specs=[part, part, whole(gq), whole(gv)],
        scratch_shapes=[pltpu.VMEM((SEQ, SEQ), BF)],
        name="unturn",
    )(seg, y, tg, gq, gv)


def run_layer(remote, seg, x, g, mats, downs, ups, norms):
    rows = x.shape[0]
    vmem, hbm = pl.BlockSpec(memory_space=pltpu.VMEM), pl.BlockSpec(memory_space=pl.ANY)
    act, grad = jax.ShapeDtypeStruct(x.shape, BF), jax.ShapeDtypeStruct((R, D), F32)
    blocks = 11
    shapes = [
        ((4, 4, 2, 3, 8, WIDE), BF),
        ((4, 4, 2, 3, 8, D), BF),
        ((4, 4, 2, 3, 8, D), BF),
        ((4, 4, 2, 3, 8, D), BF),
        ((4, 4, 2, 3, 8, FF), BF),
        ((4, 4, 2, 12, 8, D), BF),
        ((3, 8, WIDE), BF),
        ((LANES, LANES), F32),
        ((2, 2 * R, D), BF),
        ((rows, SEQ, D), BF),
        ((rows, SEQ, D), BF),
        ((SEQ, SEQ), BF),
        ((rows, SEQ, HALF), F32),
        ((rows, SEQ, 2 * R), BF),
        ((rows, SEQ, 3 * D), BF),
        ((rows, PAIRS, 2, SEQ, HALF), BF),
        ((rows, SEQ, D), BF),
        ((rows, SEQ, D), F32),
        ((rows, SEQ, 1), F32),
        ((rows, SEQ, D), BF),
        ((rows, SEQ, FF), BF),
        ((rows, SEQ, FF), BF),
        ((rows, SEQ, D), F32),
        ((rows, SEQ, D), BF),
        ((3, SEQ, 2 * LANES), BF),
    ]
    dma = pltpu.SemaphoreType.DMA
    return pl.pallas_call(
        functools.partial(layer_kernel, remote),
        out_shape=[act, act, grad, grad],
        in_specs=[vmem] * 9 + [hbm] * 8,
        out_specs=[hbm, hbm, vmem, vmem],
        scratch_shapes=[pltpu.VMEM(*s) for s in shapes]
        + [dma((blocks,)), dma((blocks, 11)), dma((blocks,)), dma((5,))]
        + [pltpu.VMEM((n, R, D), F32) for n in (2, 8)] + [pltpu.VMEM((2, 4, R, D), F32), dma((14,)), dma((14,))],
        compiler_params=pltpu.CompilerParams(
            vmem_limit_bytes=64 << 20,
            **({"collective_id": 0, "has_side_effects": True} if remote else {}),
        ),
        name="layer",
    )(seg, *ups, *norms, *downs, x, g, *mats)


def solution(mesh):
    remote = dict(mesh.shape) == {"dp": 8, "fsdp": 4}

    def body(
        tokens, segments, w_query, w_key, w_value, w_output, w_inner, w_outer, down_query, down_value,
        up_query, up_value, norm1_gain, norm1_shift, norm2_gain, norm2_shift, out_grad,
    ):
        mats = [w_query, w_key, w_value, w_output, w_inner, w_outer]
        if remote:
            mats = [m.reshape(-1, 8, m.shape[1]) for m in mats]
        else:
            pad = jnp.zeros((w_query.shape[0], LANES - 2 * R), BF)
            mats[0] = jnp.concatenate([w_query, down_query, down_value, pad], axis=1)
            mats = [lax.all_gather(m, AXES, axis=0, tiled=True) for m in mats]
            mats = [m.reshape(4, 4, 2, -1, 8, m.shape[1]) for m in mats]
        y, tg, gq, gv = run_layer(
            remote,
            segments,
            tokens,
            out_grad,
            mats,
            (down_query.T, down_value.T),
            (up_query, up_value),
            (norm1_gain, norm1_shift, norm2_gain, norm2_shift),
        )
        if not remote:
            gq, gv = lax.psum((gq, gv), AXES)
        return unturn(segments, y, tg, gq, gv)

    split, copied = P(AXES), P()
    return jax.shard_map(
        body,
        mesh=mesh,
        in_specs=(split,) * 10 + (copied,) * 6 + (split,),
        out_specs=(split, split, copied, copied),
        check_vma=False,
    )
```

```python
import functools

import jax
import jax.numpy as jnp
from jax import lax
from jax.experimental import pallas as pl
from jax.experimental.pallas import tpu as pltpu
from jax.sharding import PartitionSpec as P

MESH = pl.DeviceIdType.MESH
D, H, HD, FF, R, SEQ = 768, 12, 64, 3072, 8, 512
HALF, PAIRS, LANES = SEQ // 2, H // 2, 128
WIDE = D + LANES
BF, F32 = jnp.bfloat16, jnp.float32
AXES = ("dp", "fsdp")


def dot(a, b):
    return lax.dot_general(a, b, (((1,), (0,)), ((), ())), preferred_element_type=F32)


def dot_nt(a, b):
    return lax.dot_general(a, b, (((1,), (1,)), ((), ())), preferred_element_type=F32)


def dot_tn(a, b):
    return lax.dot_general(a, b, (((0,), (0,)), ((), ())), preferred_element_type=F32)


def mean(v):
    return jnp.mean(v, axis=-1, keepdims=True)


def gelu_parts(u):
    dens = jnp.exp2(u * u * -0.7213475204444817)
    t = 1.0 / (jnp.abs(u) * (0.3275911 * 0.7071067811865476) + 1.0)
    poly = (((0.5307027145 * t - 0.7265760135) * t + 0.7107068705) * t - 0.142248368) * t + 0.127414796
    tail = poly * t * dens
    phi = jnp.where(u < 0, tail, 1.0 - tail)
    return u * phi, phi + u * dens * 0.3989422804014327


def two_heads(v):
    first = lax.broadcasted_iota(jnp.int32, v.shape, 1) < HD
    zero = jnp.zeros_like(v)
    return jnp.concatenate([jnp.where(first, v, zero), jnp.where(first, zero, v)], axis=0)


def one_pair(v):
    first = lax.broadcasted_iota(jnp.int32, (HALF, 2 * HD), 1) < HD
    return jnp.where(first, v[:HALF], v[HALF:])


def staged(count, *stages):
    held = [None] * count
    for t in range(count + len(stages) - 1):
        for k, stage in enumerate(stages):
            if 0 <= t - k < count:
                held[t - k] = stage(t - k, held[t - k])


class Links:
    def __init__(self, groups, flat, early, ssem, rsem, lsem):
        self.early = early
        self.groups, self.flat, self.ssem, self.rsem, self.lsem = groups, flat, ssem, rsem, lsem
        dp, fs = lax.axis_index("dp"), lax.axis_index("fsdp")
        z, x, y, c = self.z, self.x, self.y, self.c = dp // 2, dp % 2, fs // 2, fs % 2
        xa, ya = jnp.where(c == 0, x, 1 - x), jnp.where(c == 0, 1 - y, y)
        xb, yb = jnp.where(c == 0, 1 - x, x), jnp.where(c == 0, y, 1 - y)
        self.near, self.far = self.device(z, xa, ya, c), self.device(z, xb, yb, c)
        self.twin, self.diag = self.device(z, x, y, 1 - c), self.device(z, 1 - x, 1 - y, c)
        self.line = [self.device((z + d) % 4, x, y, c) for d in (1, 2, 3)]
        self.up, self.down = self.device(jnp.minimum(z + 1, 3), x, y, c), self.device(jnp.maximum(z - 1, 0), x, y, c)
        self.mine, self.at_near, self.at_far, self.at_diag = x * 2 + y, xa * 2 + ya, xb * 2 + yb, 3 - x * 2 - y

    @staticmethod
    def device(z, x, y, c):
        return (z * 2 + x, y * 2 + c)

    def meet(self):
        barrier = pltpu.get_barrier_semaphore()
        others = [to for _, to in self.in_plane()] + self.on_line()[1:]
        for other in others:
            pl.semaphore_signal(barrier, 1, device_id=other, device_id_type=MESH)
        pl.semaphore_wait(barrier, len(others))

    def in_plane(self):
        there = [(n // 4, n // 2 % 2, n % 2) for n in range(1, 8)]
        place = [((self.x + i) % 2, (self.y + j) % 2, (self.c + k) % 2) for i, j, k in there]
        return [(c, self.device(self.z, x, y, c)) for x, y, c in place]

    def on_line(self):
        there = [(0, 1)] + [(d, k) for d in (1, 2, 3) for k in (0, 1)]
        return [self.device((self.z + d) % 4, self.x, self.y, (self.c + k) % 2) for d, k in there]

    def at_column(self, g, chip):
        _, buf, cols = self.groups[g]
        return buf.at[:, chip, self.c, :, :, cols]

    def at_plane(self, g, z):
        _, buf, cols = self.groups[g]
        return buf.at[z, :, self.c, :, :, cols]

    def at_piece(self, g, chip):
        _, buf, cols = self.groups[g]
        return buf.at[self.z, chip, self.c, :, :, cols]

    def send(self, g, src, dst, k, to):
        pltpu.make_async_remote_copy(
            src_ref=src,
            dst_ref=dst,
            send_sem=self.ssem.at[g],
            recv_sem=self.rsem.at[g, k],
            device_id=to,
            device_id_type=MESH,
        ).start()

    @staticmethod
    def wait(ref, sem):
        pltpu.make_async_copy(ref, ref, sem).wait()


    def own(self, g):
        src = self.groups[g][0]
        pltpu.make_async_copy(src, self.at_piece(g, self.mine), self.lsem.at[g]).start()
        for d in range(3):
            self.send(g, src, self.at_piece(g, self.mine), d, self.line[d])
        if g in self.early:
            self.send(g, src, self.at_piece(g, self.mine), 3, self.near)
            self.send(g, src, self.at_piece(g, self.mine), 4, self.far)

    def column_on(self, g, chip, *to):
        for k, other in to:
            self.send(g, self.at_column(g, chip), self.at_column(g, chip), k, other)

    def after_line(self, g):
        src = self.groups[g][0]
        self.wait(src, self.lsem.at[g])
        for d in range(3):
            self.wait(src, self.rsem.at[g, d])
        if g in self.early:
            _, buf, cols = self.groups[g]
            for k, other in ((3, self.near), (4, self.far)):
                for d in (1, 2, 3):
                    piece = buf.at[(self.z + d) % 4, self.mine, self.c, :, :, cols]
                    self.send(g, piece, piece, k, other)
            self.column_on(g, self.mine, (6, self.twin))
        else:
            self.column_on(g, self.mine, (3, self.near), (4, self.far), (6, self.twin))

    def after_near(self, g):
        self.wait(self.at_column(g, self.at_near), self.rsem.at[g, 3])
        self.column_on(g, self.at_near, (5, self.far), (7, self.twin))

    def after_far(self, g):
        self.wait(self.at_column(g, self.at_far), self.rsem.at[g, 4])
        self.column_on(g, self.at_far, (8, self.twin))

    def after_diag(self, g):
        self.wait(self.at_column(g, self.at_diag), self.rsem.at[g, 5])
        self.column_on(g, self.at_diag, (9, self.twin))

    def whole(self, g):
        for k in range(4):
            self.wait(self.at_column(g, self.mine), self.rsem.at[g, 6 + k])


    def own_flat(self, g):
        src = self.groups[g][0]
        pltpu.make_async_copy(src, self.at_piece(g, self.mine), self.lsem.at[g]).start()
        self.send(g, src, self.at_piece(g, self.mine), 0, self.near)
        self.send(g, src, self.at_piece(g, self.mine), 1, self.far)

    def near_flat(self, g):
        piece = self.at_piece(g, self.at_near)
        self.wait(piece, self.rsem.at[g, 0])
        self.send(g, piece, piece, 2, self.far)

    def plane_on(self, g, z, up, down):
        plane = self.at_plane(g, z)
        if up:
            pl.when(self.z < 3)(lambda: self.send(g, plane, plane, 3 + z, self.up))
        if down:
            pl.when(self.z > 0)(lambda: self.send(g, plane, plane, 3 + z, self.down))
        self.send(g, plane, plane, 7 + z, self.twin)

    def plane_flat(self, g):
        src = self.groups[g][0]
        self.wait(src, self.lsem.at[g])
        self.wait(src, self.rsem.at[g, 1])
        self.wait(src, self.rsem.at[g, 2])
        self.plane_on(g, self.z, True, True)

    def hop_flat(self, d, g):
        def below():
            self.wait(self.at_plane(g, self.z - d), self.rsem.at[g, 3 + self.z - d])
            self.plane_on(g, self.z - d, True, False)

        def above():
            self.wait(self.at_plane(g, self.z + d), self.rsem.at[g, 3 + self.z + d])
            self.plane_on(g, self.z + d, False, True)

        pl.when(self.z >= d)(below)
        pl.when(self.z + d <= 3)(above)

    def whole_flat(self, g):
        for z in range(4):
            self.wait(self.at_plane(g, z), self.rsem.at[g, 7 + z])

    def plan(self):
        first = [g for g in range(len(self.groups)) if g not in self.flat]
        steps = [(self.own, g) for g in first] + [(self.own_flat, g) for g in self.flat]
        stages = (self.after_line, self.after_near, self.after_far, self.after_diag, self.whole)
        main = []
        for t in range(len(first) + len(stages) - 1):
            for k, stage in enumerate(stages):
                if 0 <= t - k < len(first):
                    main.append((stage, first[t - k]))
        side = [self.near_flat, self.plane_flat] + [functools.partial(self.hop_flat, d) for d in (1, 2, 3)]
        when = ((0.12, 0.14), (0.25, 0.30), (0.45, 0.55), (0.65, 0.75), (0.85, 0.95))
        extra = [(f, (stage, g)) for stage, fs in zip(side, when) for f, g in zip(fs, self.flat)]
        for f, item in sorted(extra, key=lambda e: -e[0]):
            main.insert(int(f * len(main)), item)
        return steps, main + [(self.whole_flat, g) for g in self.flat]

    def run(self, works):
        steps, main = self.plan()
        for step, g in steps:
            step(g)
        ends = (self.whole, self.whole_flat)
        here, todo = set(), list(works)
        for step, g in main:
            if todo and todo[0][0] <= here:
                todo.pop(0)[1]()
            step(g)
            if step in ends:
                here.add(g)
        for _, fn in todo:
            fn()

    def need(self, *groups):
        pass

    def drain(self):
        for g, (src, _, _) in enumerate(self.groups):
            for _ in range(3):
                self.wait(src, self.ssem.at[g])
            if g in self.flat:
                plane = self.at_plane(g, 0)
                sent = 4 + jnp.where(self.z < 3, self.z + 1, 0) + jnp.where(self.z > 0, 4 - self.z, 0)
                lax.fori_loop(0, sent, lambda _, v: (self.wait(plane, self.ssem.at[g]), v)[1], 0)
            else:
                for _ in range(7):
                    self.wait(self.at_column(g, self.mine), self.ssem.at[g])


class Local:
    def __init__(self, groups, lsem):
        self.copies = [
            pltpu.make_async_copy(src, buf.at[:, :, :, :, :, cols], lsem.at[g]) for g, (src, buf, cols) in enumerate(groups)
        ]

    def run(self, works):
        for copy in self.copies:
            copy.start()
        here = set()
        for needs, fn in works:
            for g in sorted(needs - here):
                self.copies[g].wait()
            here |= needs
            fn()

    def need(self, *groups):
        for g in groups:
            self.copies[g].wait()

    def drain(self):
        pass


class Sums:
    def __init__(self, links, q, v, mine, plane, line, ssem, rsem):
        self.k, self.q, self.v, self.mine, self.plane, self.line = links, q, v, mine, plane, line
        self.ssem, self.rsem, self.sends = ssem, rsem, []

    def copy(self, ref, to_ref, k, to):
        send = pltpu.make_async_remote_copy(
            src_ref=ref,
            dst_ref=to_ref,
            send_sem=self.ssem.at[k],
            recv_sem=self.rsem.at[k],
            device_id=to,
            device_id_type=MESH,
        )
        send.start()
        self.sends.append(send)

    def over_plane(self):
        k = self.k
        slot = self.plane.at[(k.x * 2 + k.y) * 2 + k.c]
        self.mine[0], self.mine[1] = self.q[...], self.v[...]
        self.plane[(k.x * 2 + k.y) * 2 + k.c] = self.mine[k.c]
        for n, (core, to) in enumerate(k.in_plane()):
            self.copy(self.mine.at[core], slot, n, to)

    def end(self):
        for s in self.sends:
            s.wait()
        self.sends = []

    def over_line(self):
        self.end()
        k, p = self.k, self.plane
        self.line[k.c, k.z] = ((p[0] + p[1]) + (p[2] + p[3])) + ((p[4] + p[5]) + (p[6] + p[7]))
        places = self.line.at[k.c, k.z]
        for n, to in enumerate(k.on_line()):
            self.copy(places, places, 7 + n, to)

    def finish(self):
        p = self.line
        for n in range(7):
            pltpu.make_async_copy(p.at[0, 0], p.at[0, 0], self.rsem.at[7 + n]).wait()
            pltpu.make_async_copy(p.at[0, 0], p.at[0, 0], self.ssem.at[7 + n]).wait()
        self.q[...] = (p[0, 0] + p[0, 1]) + (p[0, 2] + p[0, 3])
        self.v[...] = (p[1, 0] + p[1, 1]) + (p[1, 2] + p[1, 3])


def find_turn(seg):
    lane = lax.broadcasted_iota(jnp.int32, (8, SEQ), 1)
    hit = (seg == pltpu.roll(seg, SEQ - HALF + 1, 1)) & (lane <= HALF)
    return jnp.min(jnp.where(hit, lane, SEQ), axis=1, keepdims=True)[0:1]


def turning(by):
    i = lax.broadcasted_iota(jnp.int32, (SEQ, SEQ), 0)
    diff = lax.broadcasted_iota(jnp.int32, (SEQ, SEQ), 1) - i - by
    return jnp.where((diff == 0) | (diff == SEQ) | (diff == -SEQ), 1.0, 0.0).astype(BF)


def layer_kernel(
    remote,
    seg_ref, up_q, up_v, g1, b1, g2, b2, dqt, dvt, x_hbm, g_hbm, wq_h, wk_h, wv_h, wo_h, win_h, wout_h,
    y_hbm, tg_hbm, gq_ref, gv_ref,
    wq_s, wk_s, wv_s, wo_s, win_s, wout_s, own_s, flip_s, up_s,
    x_s, g_s, perm_s, bias_s, low_s, qkv_s, p_s, ctx_s, n1_s, r1_s, hb_s, act_s, gp_s, dz_s, out_s, two_s,
    ssem, rsem, lsem, iosem, mine_s, plane_s, line_s, ssem2, rsem2,
):
    rows = x_s.shape[0]
    loads = [pltpu.make_async_copy(src, dst, iosem.at[k]) for k, (src, dst) in enumerate(((x_hbm, x_s), (g_hbm, g_s)))]
    for load in loads:
        load.start()

    every, col = slice(None), pl.ds
    groups = [(own_s if remote else wq_h, wq_s, every), (wk_h, wk_s, every), (wv_h, wv_s, every), (wo_h, wo_s, every)]
    lead = (every,) * (2 if remote else 5)
    groups += [(win_h.at[(*lead, col(D * j, D))], win_s, col(D * j, D)) for j in range(4)]
    groups += [(wout_h.at[(*lead, col(HALF * j, HALF))], wout_s, col(HALF * j, HALF)) for j in range(3)]
    wq_g, wk_g, wv_g, wo_g, win_g, wout_g = 0, 1, 2, 3, 4, 8

    if remote:
        stage = pltpu.make_async_copy(wq_h, own_s.at[:, :, col(0, D)], iosem.at[2])
        stage.start()
        flip_s[...] = jnp.zeros_like(flip_s)
        flip_s[0:R, 0 : dqt.shape[1]] = dqt[...].astype(F32)
        flip_s[R : 2 * R, 0 : dvt.shape[1]] = dvt[...].astype(F32)
        downs = flip_s[...].T[0 : dqt.shape[1]].astype(BF)
        own_s[:, :, D:] = downs.reshape(*own_s.shape[:2], LANES)
        net = Links(groups, (wout_g + 1, wout_g + 2), (0, 1, 2, 3, 4), ssem, rsem, lsem)
        net.meet()
        stage.wait()
    else:
        net = Local(groups, lsem)
    zeros = jnp.zeros((R, D), F32)
    up_s[0] = jnp.concatenate([2.0 * up_q[...].astype(F32), zeros], axis=0).astype(BF)
    up_s[1] = jnp.concatenate([zeros, 2.0 * up_v[...].astype(F32)], axis=0).astype(BF)
    gq_ref[...] = jnp.zeros_like(gq_ref)
    gv_ref[...] = jnp.zeros_like(gv_ref)

    def flat(ref, cols=every):
        v = ref[:, :, :, :, :, cols]
        return v.reshape(-1, v.shape[-1])

    def thirds(fn):
        for n in range(3):
            fn(slice(HALF * n, HALF * (n + 1)))

    def each_row(fn, *args):
        def one(r, carry):
            fn(r, *args)
            return carry

        return lambda: lax.fori_loop(0, rows, one, 0)

    def each_half(fn, *args):
        def one(t, carry):
            fn(t // 2, pl.ds(pl.multiple_of(HALF * (t % 2), HALF), HALF), *args)
            return carry

        return lambda: lax.fori_loop(0, 2 * rows, one, 0)

    def turn(r):
        seg = jnp.broadcast_to(seg_ref[pl.ds(r, 1), :], (8, SEQ))
        perm_s[...] = turning(find_turn(seg))
        segb = seg.astype(F32).astype(BF)
        seg_row = dot_nt(perm_s[HALF:, :], segb)[:, 0:1]
        seg_col = dot_nt(segb, perm_s[HALF:, :])[0:1]
        bias = jnp.where(seg_col == seg_row, 0.0, -1e30)
        bias_s[r, :HALF] = bias
        bias_s[r, HALF:] = bias

        def part(c):
            x_s[r, :, c] = dot(perm_s[...], x_s[r, :, c]).astype(BF)
            g_s[r, :, c] = dot(perm_s[...], g_s[r, :, c]).astype(BF)

        thirds(part)

    def first_turn():
        for load in loads:
            load.wait()
        each_row(turn)()

    def project(r):
        low_s[r] = dot(x_s[r], flat(wq_s, slice(D, D + 2 * R))).astype(BF)

        def part(c):
            qkv_s[r, :, c] = (dot(x_s[r], flat(wq_s, c)) + dot(low_s[r], up_s[0, :, c])).astype(BF)

        thirds(part)

    def project_k(r):
        def part(c):
            qkv_s[r, :, D + c.start : D + c.stop] = dot(x_s[r], flat(wk_s, c)).astype(BF)

        thirds(part)

    def project_v(r):
        def part(c):
            v = dot(x_s[r], flat(wv_s, c)) + dot(low_s[r], up_s[1, :, c])
            qkv_s[r, :, 2 * D + c.start : 2 * D + c.stop] = v.astype(BF)

        thirds(part)

    def item(i, n):
        p, b = 2 * i + n // 2, n % 2
        return p, b, slice(HALF * b, HALF * (b + 1)), [pl.ds(pl.multiple_of(D * w + LANES * p, LANES), LANES) for w in range(3)]

    def heads(r):
        def some(i, carry):
            def scores(n, _):
                p, b, span, cut = item(i, n)
                s = dot_nt(two_heads(qkv_s[r, span, cut[0]] * 0.125), qkv_s[r, span, cut[1]])
                return s + bias_s[r] if b == 1 else s

            def soften(n, s):
                p, b, _, _ = item(i, n)
                e = jnp.exp(s - jnp.max(s, axis=1, keepdims=True))
                probs = (e * (1.0 / jnp.sum(e, axis=1, keepdims=True))).astype(BF)
                p_s[r, p, b] = probs
                return probs

            def context(n, probs):
                p, b, span, cut = item(i, n)
                ctx_s[r, span, cut[0]] = one_pair(dot(probs, qkv_s[r, span, cut[2]])).astype(BF)

            staged(4, scores, soften, context)
            return carry

        lax.fori_loop(0, PAIRS // 2, some, 0)

    def attended(r):
        z1 = x_s[r].astype(F32) + dot(ctx_s[r], flat(wo_s))
        z1 = z1 - mean(z1)
        r1 = lax.rsqrt(mean(z1 * z1) + 1e-5)
        n1 = z1 * r1
        n1_s[r] = n1
        r1_s[r] = r1
        hb_s[r] = (n1 * g1[...][None] + b1[...][None]).astype(BF)

    def inner(r, j):
        for n in range(3):
            c = slice(D * j + HALF * n, D * j + HALF * (n + 1))
            act, slope = gelu_parts(dot(hb_s[r], flat(win_s, c)))
            act_s[r, :, c] = act.astype(BF)
            gp_s[r, :, c] = slope.astype(BF)

    def outer(r, span, j):
        c = slice(HALF * j, HALF * (j + 1))
        return n1_s[r, span, c] * g1[...][None, c] + b1[...][None, c] + dot(act_s[r, span], flat(wout_s, c))

    def back(r):
        spans = [slice(HALF * b, HALF * (b + 1)) for b in range(2)]

        def summed(b, _):
            return [outer(r, spans[b], j) for j in range(3)]

        def second_norm(b, last):
            span = spans[b]
            z2 = jnp.concatenate(last, axis=1)
            z2 = z2 - mean(z2)
            r2 = lax.rsqrt(mean(z2 * z2) + 1e-5)
            n2 = z2 * r2
            out_s[r, span] = (n2 * g2[...][None] + b2[...][None]).astype(BF)
            pltpu.make_async_copy(out_s.at[r, span], y_hbm.at[r, span], iosem.at[3]).start()
            dn2 = g_s[r, span].astype(F32) * g2[...][None]
            dz2 = r2 * (dn2 - mean(dn2) - n2 * mean(dn2 * n2))
            dz_s[r, span] = dz2
            return dz2.astype(BF)

        def inner_back(b, df):
            for n in range(4):
                c = slice(D * n, D * (n + 1))
                dact = dot_nt(df, wout_s[n].reshape(D, D))
                act_s[r, spans[b], c] = (dact * gp_s[r, spans[b], c].astype(F32)).astype(BF)

        def hidden_back(b, _):
            return dot_nt(act_s[r, spans[b]], flat(win_s))

        def first_norm(b, dh):
            span = spans[b]
            dn1 = (dz_s[r, span] + dh) * g1[...][None]
            n1 = n1_s[r, span]
            dz1 = r1_s[r, span] * (dn1 - mean(dn1) - n1 * mean(dn1 * n1))
            dz_s[r, span] = dz1
            return dz1.astype(BF)

        def context_back(b, dz1):
            ctx_s[r, spans[b]] = dot_nt(dz1, flat(wo_s)).astype(BF)

        staged(2, summed, second_norm, inner_back, hidden_back, first_norm, context_back)

    def heads_back(t, carry):
        r, i = t // (PAIRS // 2), t % (PAIRS // 2)

        def to(n):
            return slice(HALF * (n % 2), HALF * (n % 2 + 1)), slice(LANES * (n // 2), LANES * (n // 2 + 1))

        def values(n, _):
            p, b, span, cut = item(i, n)
            dc = two_heads(ctx_s[r, span, cut[0]])
            dp = dot_nt(dc, qkv_s[r, span, cut[2]])
            two_s[2, *to(n)] = dot_tn(dc, p_s[r, p, b]).T.astype(BF)
            return dp

        def scores(n, dp):
            p, b, _, _ = item(i, n)
            probs = p_s[r, p, b].astype(F32)
            return (probs * (dp - jnp.sum(probs * dp, axis=1, keepdims=True))).astype(BF)

        def sides(n, ds):
            p, b, span, cut = item(i, n)
            two_s[0, *to(n)] = (one_pair(dot(ds, qkv_s[r, span, cut[1]])) * 0.125).astype(BF)
            p_s[r, p, b] = ds

        staged(4, values, scores, sides)
        hb_s[r, :, pl.ds(pl.multiple_of(2 * LANES * i, LANES), 2 * LANES)] = two_s[0]
        qkv_s[r, :, pl.ds(pl.multiple_of(2 * D + 2 * LANES * i, LANES), 2 * LANES)] = two_s[2]
        return carry

    def keys_back(t, carry):
        r, i = t // (PAIRS // 2), t % (PAIRS // 2)
        for n in range(4):
            p, b, span, cut = item(i, n)
            dk = dot_tn(two_heads(qkv_s[r, span, cut[0]] * 0.125), p_s[r, p, b]).T.astype(BF)
            two_s[1, span, LANES * (n // 2) : LANES * (n // 2 + 1)] = dk
        qkv_s[r, :, pl.ds(pl.multiple_of(D + 2 * LANES * i, LANES), 2 * LANES)] = two_s[1]
        return carry

    def grads(r):
        gq_ref[...] += 2.0 * dot_tn(low_s[r], hb_s[r])[:R]
        gv_ref[...] += 2.0 * dot_tn(low_s[r], qkv_s[r, :, 2 * D :])[R:]

    def tokens_back(r, span):
        dq, dk, dv = hb_s[r, span], qkv_s[r, span, D : 2 * D], qkv_s[r, span, 2 * D :]
        dlow = (dot_nt(dq, up_s[0]) + dot_nt(dv, up_s[1])).astype(BF)
        tg = dz_s[r, span] + dot_nt(dq, flat(wq_s, slice(0, D))) + dot_nt(dk, flat(wk_s)) + dot_nt(dv, flat(wv_s))
        out_s[r, span] = (tg + dot_nt(dlow, flat(wq_s, slice(D, D + 2 * R)))).astype(BF)
        pltpu.make_async_copy(out_s.at[r, span], tg_hbm.at[r, span], iosem.at[4]).start()

    works = [
        (set(), first_turn),
        ({wq_g}, each_row(project)),
        ({wk_g}, each_row(project_k)),
        ({wv_g}, each_row(project_v)),
    ]
    works += [({wv_g}, functools.partial(heads, r)) for r in range(rows)]
    works += [({wo_g}, each_row(attended))]
    works += [({win_g + j}, functools.partial(inner, r, j)) for j in range(4) for r in range(rows)]
    net.run(works)
    net.need(wout_g, wout_g + 1, wout_g + 2)
    each_row(back)()
    lax.fori_loop(0, rows * PAIRS // 2, heads_back, 0)
    each_row(grads)()
    pltpu.make_async_copy(out_s, y_hbm, iosem.at[3]).wait()
    if remote:
        sums = Sums(net, gq_ref, gv_ref, mine_s, plane_s, line_s, ssem2, rsem2)
        sums.over_plane()
        lax.fori_loop(0, rows * PAIRS // 2, keys_back, 0)
        sums.over_line()
        each_half(tokens_back)()
        net.drain()
        sums.finish()
    else:
        lax.fori_loop(0, rows * PAIRS // 2, keys_back, 0)
        each_half(tokens_back)()
    pltpu.make_async_copy(out_s, tg_hbm, iosem.at[4]).wait()


def unturn_kernel(seg_ref, y_ref, tg_ref, gq_ref, gv_ref, oy_ref, otg_ref, oq_ref, ov_ref, perm_s):
    perm_s[...] = turning(-find_turn(jnp.broadcast_to(seg_ref[pl.ds(pl.program_id(0), 1), :], (8, SEQ))))
    oy_ref[0] = dot(perm_s[...], y_ref[0]).astype(BF)
    otg_ref[0] = dot(perm_s[...], tg_ref[0]).astype(BF)
    oq_ref[...] = gq_ref[...]
    ov_ref[...] = gv_ref[...]


def unturn(seg, y, tg, gq, gv):
    def whole(v):
        return pl.BlockSpec(v.shape, lambda r: (0, 0))

    part = pl.BlockSpec((1, SEQ, D), lambda r: (r, 0, 0))
    act, grad = jax.ShapeDtypeStruct(y.shape, BF), jax.ShapeDtypeStruct(gq.shape, F32)
    return pl.pallas_call(
        unturn_kernel,
        grid=(y.shape[0],),
        out_shape=[act, act, grad, grad],
        in_specs=[whole(seg), part, part, whole(gq), whole(gv)],
        out_specs=[part, part, whole(gq), whole(gv)],
        scratch_shapes=[pltpu.VMEM((SEQ, SEQ), BF)],
        name="unturn",
    )(seg, y, tg, gq, gv)


def run_layer(remote, seg, x, g, mats, downs, ups, norms):
    rows = x.shape[0]
    vmem, hbm = pl.BlockSpec(memory_space=pltpu.VMEM), pl.BlockSpec(memory_space=pl.ANY)
    act, grad = jax.ShapeDtypeStruct(x.shape, BF), jax.ShapeDtypeStruct((R, D), F32)
    blocks = 11
    shapes = [
        ((4, 4, 2, 3, 8, WIDE), BF),
        ((4, 4, 2, 3, 8, D), BF),
        ((4, 4, 2, 3, 8, D), BF),
        ((4, 4, 2, 3, 8, D), BF),
        ((4, 4, 2, 3, 8, FF), BF),
        ((4, 4, 2, 12, 8, D), BF),
        ((3, 8, WIDE), BF),
        ((LANES, LANES), F32),
        ((2, 2 * R, D), BF),
        ((rows, SEQ, D), BF),
        ((rows, SEQ, D), BF),
        ((SEQ, SEQ), BF),
        ((rows, SEQ, HALF), F32),
        ((rows, SEQ, 2 * R), BF),
        ((rows, SEQ, 3 * D), BF),
        ((rows, PAIRS, 2, SEQ, HALF), BF),
        ((rows, SEQ, D), BF),
        ((rows, SEQ, D), F32),
        ((rows, SEQ, 1), F32),
        ((rows, SEQ, D), BF),
        ((rows, SEQ, FF), BF),
        ((rows, SEQ, FF), BF),
        ((rows, SEQ, D), F32),
        ((rows, SEQ, D), BF),
        ((3, SEQ, 2 * LANES), BF),
    ]
    dma = pltpu.SemaphoreType.DMA
    return pl.pallas_call(
        functools.partial(layer_kernel, remote),
        out_shape=[act, act, grad, grad],
        in_specs=[vmem] * 9 + [hbm] * 8,
        out_specs=[hbm, hbm, vmem, vmem],
        scratch_shapes=[pltpu.VMEM(*s) for s in shapes]
        + [dma((blocks,)), dma((blocks, 11)), dma((blocks,)), dma((5,))]
        + [pltpu.VMEM((n, R, D), F32) for n in (2, 8)] + [pltpu.VMEM((2, 4, R, D), F32), dma((14,)), dma((14,))],
        compiler_params=pltpu.CompilerParams(
            vmem_limit_bytes=64 << 20,
            **({"collective_id": 0, "has_side_effects": True} if remote else {}),
        ),
        name="layer",
    )(seg, *ups, *norms, *downs, x, g, *mats)


def solution(mesh):
    remote = dict(mesh.shape) == {"dp": 8, "fsdp": 4}

    def body(
        tokens, segments, w_query, w_key, w_value, w_output, w_inner, w_outer, down_query, down_value,
        up_query, up_value, norm1_gain, norm1_shift, norm2_gain, norm2_shift, out_grad,
    ):
        mats = [w_query, w_key, w_value, w_output, w_inner, w_outer]
        if remote:
            mats = [m.reshape(-1, 8, m.shape[1]) for m in mats]
        else:
            pad = jnp.zeros((w_query.shape[0], LANES - 2 * R), BF)
            mats[0] = jnp.concatenate([w_query, down_query, down_value, pad], axis=1)
            mats = [lax.all_gather(m, AXES, axis=0, tiled=True) for m in mats]
            mats = [m.reshape(4, 4, 2, -1, 8, m.shape[1]) for m in mats]
        y, tg, gq, gv = run_layer(
            remote,
            segments,
            tokens,
            out_grad,
            mats,
            (down_query.T, down_value.T),
            (up_query, up_value),
            (norm1_gain, norm1_shift, norm2_gain, norm2_shift),
        )
        if not remote:
            gq, gv = lax.psum((gq, gv), AXES)
        return unturn(segments, y, tg, gq, gv)

    split, copied = P(AXES), P()
    return jax.shard_map(
        body,
        mesh=mesh,
        in_specs=(split,) * 10 + (copied,) * 6 + (split,),
        out_specs=(split, split, copied, copied),
        check_vma=False,
    )
```
